32 devices in a mesh: dp: 8 (over y, x, core), head: 4 (over z).
Axes of the slice: x: 2, y: 2, z: 4, core: 2. Of those that a mesh axis runs over, the one named last changes fastest.
Arguments:
- block_input: bfloat16 [512, 50, 512], P(('dp', 'head')), may hold values from -6 to 6
- out_grad: bfloat16 [512, 50, 512], P(('dp', 'head')), may hold values from -6 to 6
- kernel_radius: int32 [8], replicated, may hold values from 1 to 3, as said below
- qkv_weight: float32 [512, 3, 512], P('dp', None, 'head'), may hold values from -0.25 to 0.25
- qkv_first: float32 [512, 3, 512], P('dp', None, 'head'), may hold values from -0.0004 to 0.0004
- qkv_second: float32 [512, 3, 512], P('dp', None, 'head'), may hold values from 3e-10 to 1.3e-09
- qkv_average: float32 [512, 3, 512], P('dp', None, 'head'), may hold values from -0.25 to 0.25
- proj_weight: float32 [512, 512], P('dp', 'head'), may hold values from -0.25 to 0.25
- proj_first: float32 [512, 512], P('dp', 'head'), may hold values from -0.0004 to 0.0004
- proj_second: float32 [512, 512], P('dp', 'head'), may hold values from 3e-10 to 1.3e-09
- proj_average: float32 [512, 512], P('dp', 'head'), may hold values from -0.25 to 0.25
- up_weight: float32 [512, 2048], P('dp', 'head'), may hold values from -0.25 to 0.25
- up_first: float32 [512, 2048], P('dp', 'head'), may hold values from -0.0004 to 0.0004
- up_second: float32 [512, 2048], P('dp', 'head'), may hold values from 3e-10 to 1.3e-09
- up_average: float32 [512, 2048], P('dp', 'head'), may hold values from -0.25 to 0.25
- down_weight: float32 [512, 2048], P('dp', 'head'), may hold values from -0.125 to 0.125
- down_first: float32 [512, 2048], P('dp', 'head'), may hold values from -0.0004 to 0.0004
- down_second: float32 [512, 2048], P('dp', 'head'), may hold values from 3e-10 to 1.3e-09
- down_average: float32 [512, 2048], P('dp', 'head'), may hold values from -0.125 to 0.125
- head_params: float32 [56, 512], replicated, may hold values from -1.2 to 1.2
- head_first: float32 [56, 512], replicated, may hold values from -0.0015 to 0.0015
- head_second: float32 [56, 512], replicated, may hold values from 5e-09 to 2e-08
- head_average: float32 [56, 512], replicated, may hold values from -1.2 to 1.2
- rep_params: float32 [16, 512], replicated, may hold values from -1.2 to 1.4, as said below
- rep_first: float32 [16, 512], replicated, may hold values from -0.0015 to 0.0015
- rep_second: float32 [16, 512], replicated, may hold values from 5e-09 to 2e-08
- rep_average: float32 [16, 512], replicated, may hold values from -1.8 to 1.8
Outputs:
- block_output: bfloat16 [512, 50, 512], P(('dp', 'head'))
- input_grad: bfloat16 [512, 50, 512], P(('dp', 'head'))
- grad_norm: float32 [], replicated
- qkv_grad: float32 [512, 3, 512], P('dp', None, 'head')
- qkv_first_new: float32 [512, 3, 512], P('dp', None, 'head')
- qkv_second_new: float32 [512, 3, 512], P('dp', None, 'head')
- qkv_weight_new: float32 [512, 3, 512], P('dp', None, 'head')
- qkv_weight_low: bfloat16 [512, 3, 512], P('dp', None, 'head')
- qkv_average_new: float32 [512, 3, 512], P('dp', None, 'head')
- proj_grad: float32 [512, 512], P('dp', 'head')
- proj_first_new: float32 [512, 512], P('dp', 'head')
- proj_second_new: float32 [512, 512], P('dp', 'head')
- proj_weight_new: float32 [512, 512], P('dp', 'head')
- proj_weight_low: bfloat16 [512, 512], P('dp', 'head')
- proj_average_new: float32 [512, 512], P('dp', 'head')
- up_grad: float32 [512, 2048], P('dp', 'head')
- up_first_new: float32 [512, 2048], P('dp', 'head')
- up_second_new: float32 [512, 2048], P('dp', 'head')
- up_weight_new: float32 [512, 2048], P('dp', 'head')
- up_weight_low: bfloat16 [512, 2048], P('dp', 'head')
- up_average_new: float32 [512, 2048], P('dp', 'head')
- down_grad: float32 [512, 2048], P('dp', 'head')
- down_first_new: float32 [512, 2048], P('dp', 'head')
- down_second_new: float32 [512, 2048], P('dp', 'head')
- down_weight_new: float32 [512, 2048], P('dp', 'head')
- down_weight_low: bfloat16 [512, 2048], P('dp', 'head')
- down_average_new: float32 [512, 2048], P('dp', 'head')
- head_grad: float32 [56, 512], replicated
- head_first_new: float32 [56, 512], replicated
- head_second_new: float32 [56, 512], replicated
- head_weight_new: float32 [56, 512], replicated
- head_weight_low: bfloat16 [56, 512], replicated
- head_average_new: float32 [56, 512], replicated
- rep_grad: float32 [16, 512], replicated
- rep_first_new: float32 [16, 512], replicated
- rep_second_new: float32 [16, 512], replicated
- rep_weight_new: float32 [16, 512], replicated
- rep_weight_low: bfloat16 [16, 512], replicated
- rep_average_new: float32 [16, 512], replicated
The draws below stay inside these ranges and needn't reach their ends.
Inputs may be any that keep to these rules, and one draw needn't show every extreme that they name: `kernel_radius`: two heads have radius 1, three radius 2 and three radius 3; which heads is drawn. `rep_params`: rows 10 and 12 are gains near 1; the other rows are of order 0.2.
All inputs are finite; a program needn't handle non-finite values.
Results may differ from the reference program's by a relative error of at most 0.014.
Values may be sent and summed in bfloat16 or wider, within the bound.
No kernel may reach another device: no remote copies, remote signals or barrier semaphores. Data moves between devices by JAX's collectives and lax.ppermute only.
A program may use at most 192 MiB of HBM per device.

```python
import math
import jax
import jax.numpy as jnp
from jax import lax

D = 512
HEADS = 8
HD = 64
FF = 2048
GRID = 7
TAPS = 49
STEP = 5
IMG_DEV = 16
SEQ = 50
IMAGES = 512


def draw_kernel_radius(key, part):
    order = jax.random.permutation(key, HEADS)
    return (1 + (order >= 2).astype(jnp.int32) + (order >= 5).astype(jnp.int32)).astype(jnp.int32)


def draw_rep_params(key, part):
    base = jax.random.normal(key, (16, D), jnp.float32)
    rows_index = lax.broadcasted_iota(jnp.int32, (16, D), 0)
    gains = (rows_index == 10) | (rows_index == 12)
    return jnp.where(gains, 1.0 + 0.1 * jnp.clip(base, -4.0, 4.0), 0.2 * jnp.clip(base, -6.0, 6.0)).astype(jnp.float32)


def block_levels(rng, dims, shards, low, high):
    factor_of, own = 1.0, jax.random.fold_in(rng, 6)
    for dim, blocks in shards:
        draws = jnp.exp(jax.random.uniform(jax.random.fold_in(own, dim), (blocks,), jnp.float32, low / len(shards), high / len(shards)))
        factor_of = factor_of * jnp.repeat(draws, dims[dim] // blocks).reshape([-1 if axis == dim else 1 for axis in range(len(dims))])
    return factor_of


def bell_draw(key, shape, deviation, most, shards=(), dtype=jnp.bfloat16):
    entries = deviation * jax.random.normal(key, shape, jnp.float32)
    if shards:
        entries = entries * block_levels(key, shape, shards, -0.22, 0.18)
    return jnp.clip(entries, -most, most).astype(dtype)


def setup_inputs(seed: int = 0) -> dict:
    keys = jax.random.split(jax.random.key(seed), 28)
    block_input = bell_draw(keys[0], (IMAGES, SEQ, D), 1.0, 6.0, ((0, 32),))
    out_grad = bell_draw(keys[1], (IMAGES, SEQ, D), 1.0, 6.0, ((0, 32),))
    kernel_radius = draw_kernel_radius(jax.random.fold_in(keys[27], 71), 0)
    qkv_weight = bell_draw(keys[3], (D, 3, D), D ** -0.5, 0.25, ((0, 8), (2, 4)), jnp.float32)
    qkv_first = bell_draw(keys[4], (D, 3, D), 0.00006, 0.0004, ((0, 8), (2, 4)), jnp.float32)
    qkv_second = jnp.clip(jnp.exp(math.log(1.2999999965401798e-09) - 1.4663371 * jax.random.uniform(keys[5], (D, 3, D), jnp.float32) ** block_levels(keys[5], (D, 3, D), ((0, 8), (2, 4)), -0.2, 0.2)), 2.999999970665357e-10, 1.2999999965401798e-09)
    qkv_average = bell_draw(keys[6], (D, 3, D), D ** -0.5, 0.25, ((0, 8), (2, 4)), jnp.float32)
    proj_weight = bell_draw(keys[7], (D, D), D ** -0.5, 0.25, ((0, 8), (1, 4)), jnp.float32)
    proj_first = bell_draw(keys[8], (D, D), 0.00006, 0.0004, ((0, 8), (1, 4)), jnp.float32)
    proj_second = jnp.clip(jnp.exp(math.log(1.2999999965401798e-09) - 1.4663371 * jax.random.uniform(keys[9], (D, D), jnp.float32) ** block_levels(keys[9], (D, D), ((0, 8), (1, 4)), -0.2, 0.2)), 2.999999970665357e-10, 1.2999999965401798e-09)
    proj_average = bell_draw(keys[10], (D, D), D ** -0.5, 0.25, ((0, 8), (1, 4)), jnp.float32)
    up_weight = bell_draw(keys[11], (D, FF), D ** -0.5, 0.25, ((0, 8), (1, 4)), jnp.float32)
    up_first = bell_draw(keys[12], (D, FF), 0.00006, 0.0004, ((0, 8), (1, 4)), jnp.float32)
    up_second = jnp.clip(jnp.exp(math.log(1.2999999965401798e-09) - 1.4663371 * jax.random.uniform(keys[13], (D, FF), jnp.float32) ** block_levels(keys[13], (D, FF), ((0, 8), (1, 4)), -0.2, 0.2)), 2.999999970665357e-10, 1.2999999965401798e-09)
    up_average = bell_draw(keys[14], (D, FF), D ** -0.5, 0.25, ((0, 8), (1, 4)), jnp.float32)
    down_weight = bell_draw(keys[15], (D, FF), FF ** -0.5, 0.125, ((0, 8), (1, 4)), jnp.float32)
    down_first = bell_draw(keys[16], (D, FF), 0.00006, 0.0004, ((0, 8), (1, 4)), jnp.float32)
    down_second = jnp.clip(jnp.exp(math.log(1.2999999965401798e-09) - 1.4663371 * jax.random.uniform(keys[17], (D, FF), jnp.float32) ** block_levels(keys[17], (D, FF), ((0, 8), (1, 4)), -0.2, 0.2)), 2.999999970665357e-10, 1.2999999965401798e-09)
    down_average = bell_draw(keys[18], (D, FF), FF ** -0.5, 0.125, ((0, 8), (1, 4)), jnp.float32)
    head_params = bell_draw(keys[19], (TAPS + 3 + FF // D, D), 0.2, 1.2, (), jnp.float32)
    head_first = bell_draw(keys[20], (TAPS + 3 + FF // D, D), 0.00022, 0.0015, (), jnp.float32)
    head_second = jnp.clip(jnp.exp(jax.random.uniform(keys[21], (TAPS + 3 + FF // D, D), jnp.float32, math.log(4.999999969612645e-09), math.log(1.999999987845058e-08))), 4.999999969612645e-09, 1.999999987845058e-08)
    head_average = bell_draw(keys[22], (TAPS + 3 + FF // D, D), 0.2, 1.2, (), jnp.float32)
    rep_params = draw_rep_params(jax.random.fold_in(keys[27], 71), 0)
    rep_first = bell_draw(keys[24], (16, D), 0.00022, 0.0015, (), jnp.float32)
    rep_second = jnp.clip(jnp.exp(jax.random.uniform(keys[25], (16, D), jnp.float32, math.log(4.999999969612645e-09), math.log(1.999999987845058e-08))), 4.999999969612645e-09, 1.999999987845058e-08)
    rep_average = bell_draw(keys[26], (16, D), 0.3, 1.8, (), jnp.float32)
    return dict(block_input=block_input, out_grad=out_grad, kernel_radius=kernel_radius, qkv_weight=qkv_weight, qkv_first=qkv_first, qkv_second=qkv_second, qkv_average=qkv_average, proj_weight=proj_weight, proj_first=proj_first, proj_second=proj_second, proj_average=proj_average, up_weight=up_weight, up_first=up_first, up_second=up_second, up_average=up_average, down_weight=down_weight, down_first=down_first, down_second=down_second, down_average=down_average, head_params=head_params, head_first=head_first, head_second=head_second, head_average=head_average, rep_params=rep_params, rep_first=rep_first, rep_second=rep_second, rep_average=rep_average)


@jax.custom_vjp
def low(v):
    return lax.optimization_barrier(v.astype(jnp.bfloat16)).astype(jnp.float32)

@jax.custom_vjp
def low_back(v):
    return v

def low_keep(v):
    return (low(v), None)

def low_pass(kept, grad):
    return (grad,)

def back_keep(v):
    return (v, None)

def back_low(kept, grad):
    return (low(grad),)
low.defvjp(low_keep, low_pass)
low_back.defvjp(back_keep, back_low)
NORM_EPS = 1e-06
BETA_FIRST = 0.9
BETA_SECOND = 0.999
ADAM_EPS = 1e-08
LEARN_RATE = 0.1
WEIGHT_DECAY = 0.05
CLIP_NORM = 1.0
AVG_KEEP = 0.9
HIGHEST = lax.Precision.HIGHEST

def tap_mask(radius):
    reach = jnp.repeat(radius, HD)
    taps = lax.broadcasted_iota(jnp.int32, (TAPS, reach.shape[0]), 0)
    vertical = jnp.abs(taps // 7 - 3)
    horizontal = jnp.abs(taps % 7 - 3)
    inside = (vertical <= reach[None, :]) & (horizontal <= reach[None, :])
    return inside.astype(jnp.float32)

def depthwise(grid, taps, reach):
    side = 2 * reach + 1
    extent = grid.shape[1]
    padded = jnp.pad(grid, ((0, 0), (reach, reach), (reach, reach), (0, 0)))
    total = jnp.zeros(grid.shape, jnp.float32)
    for tap_row in range(side):
        for tap_col in range(side):
            total = total + taps[tap_row * side + tap_col] * padded[:, tap_row:tap_row + extent, tap_col:tap_col + extent, :]
    return total

def layer_norm(values, gain, shift):
    center = values - lax.optimization_barrier(jnp.mean(values, axis=-1, keepdims=True))
    scale_inv = lax.rsqrt(lax.optimization_barrier(jnp.mean(center * center, axis=-1, keepdims=True)) + NORM_EPS)
    return center * scale_inv * gain + shift

def soft_tokens(scores):
    top = lax.optimization_barrier(jnp.max(scores, axis=1, keepdims=True))
    expo = jnp.exp(scores - top)
    return expo / lax.optimization_barrier(jnp.sum(expo, axis=1, keepdims=True))

def forward(values, w_qkv, w_proj, w_up, w_down, head_par, rep_par, mask):
    images = values.shape[0]
    cls_part = values[:, :1]
    pixels = values[:, 1:].reshape(images, GRID, GRID, D)
    mixed = pixels + depthwise(pixels, rep_par[0:9], 1) + rep_par[9]
    stream_zero = jnp.concatenate([cls_part, mixed.reshape(images, GRID * GRID, D)], axis=1)
    normed_one = low(layer_norm(stream_zero, rep_par[10], rep_par[11]))
    bias_qkv = jnp.stack([head_par[TAPS + 1], jnp.zeros((D,), jnp.float32), head_par[TAPS + 2]])
    proj_qkv = low_back(jnp.einsum('bnd,dte->bnte', normed_one, low(w_qkv), precision=HIGHEST) + bias_qkv)
    queries = proj_qkv[:, :, 0]
    keys_raw = proj_qkv[:, :, 1]
    values_v = proj_qkv[:, :, 2]
    keys_soft = soft_tokens(keys_raw)
    query_heads = queries.reshape(images, SEQ, HEADS, HD)
    key_heads = keys_soft.reshape(images, SEQ, HEADS, HD)
    value_heads = values_v.reshape(images, SEQ, HEADS, HD)
    context = jnp.einsum('bnhi,bnhj->bhij', key_heads, value_heads, precision=HIGHEST)
    factor = HD ** (-0.5) * jnp.einsum('bnhi,bhij->bnhj', query_heads, context, precision=HIGHEST).reshape(images, SEQ, D)
    value_grid = values_v[:, 1:].reshape(images, GRID, GRID, D)
    conv_val = depthwise(value_grid, head_par[0:TAPS] * mask, 3) + head_par[TAPS]
    encoded = queries[:, 1:] * conv_val.reshape(images, GRID * GRID, D)
    attended = low(factor + jnp.concatenate([jnp.zeros((images, 1, D), jnp.float32), encoded], axis=1))
    proj_out = low_back(jnp.einsum('bnc,oc->bno', attended, low(w_proj), precision=HIGHEST) + rep_par[14])
    stream_one = stream_zero + proj_out
    normed_two = low(layer_norm(stream_one, rep_par[12], rep_par[13]))
    up_bias = head_par[TAPS + 3:].reshape(FF)
    hidden_pre = low_back(jnp.einsum('bnd,df->bnf', normed_two, low(w_up), precision=HIGHEST) + up_bias)
    hidden = low(jax.nn.gelu(hidden_pre, approximate=False))
    return stream_one + jnp.einsum('bnf,df->bnd', hidden, low(w_down), precision=HIGHEST) + rep_par[15]

def adam_step(raw, weight, first, second, average, scale_clip, decay):
    grad = raw * scale_clip
    first_new = BETA_FIRST * first + (1.0 - BETA_FIRST) * grad
    second_new = BETA_SECOND * second + (1.0 - BETA_SECOND) * grad * grad
    moment_hat = first_new / (1.0 - BETA_FIRST ** STEP)
    second_hat = second_new / (1.0 - BETA_SECOND ** STEP)
    weight_new = weight - LEARN_RATE * (moment_hat / (jnp.sqrt(second_hat) + ADAM_EPS) + decay * weight)
    average_new = AVG_KEEP * average + (1.0 - AVG_KEEP) * weight_new
    return (grad, first_new, second_new, weight_new, weight_new.astype(jnp.bfloat16), average_new)

def reference(block_input, out_grad, kernel_radius, qkv_weight, qkv_first, qkv_second, qkv_average, proj_weight, proj_first, proj_second, proj_average, up_weight, up_first, up_second, up_average, down_weight, down_first, down_second, down_average, head_params, head_first, head_second, head_average, rep_params, rep_first, rep_second, rep_average):
    mask = tap_mask(kernel_radius)
    params = (qkv_weight, proj_weight, up_weight, down_weight, head_params, rep_params)
    blocks = IMAGES // IMG_DEV
    inputs = block_input.astype(jnp.float32).reshape(blocks, IMG_DEV, SEQ, D)
    cotangents = out_grad.astype(jnp.float32).reshape(blocks, IMG_DEV, SEQ, D)

    def forward_masked(values, w_qkv, w_proj, w_up, w_down, head_par, rep_par):
        return forward(values, w_qkv, w_proj, w_up, w_down, head_par, rep_par, mask)

    def scan_step(carry, pair):
        out_val, pull = jax.vjp(forward_masked, pair[0], *params)
        pulled = pull(pair[1])
        carry = tuple((acc + part for acc, part in zip(carry, pulled[1:])))
        return (carry, (out_val.astype(jnp.bfloat16), pulled[0].astype(jnp.bfloat16)))
    zeros = tuple((jnp.zeros(item.shape, jnp.float32) for item in params))
    sums, (outputs, grads_in) = lax.scan(scan_step, zeros, (inputs, cotangents))
    block_output = outputs.reshape(IMAGES, SEQ, D)
    input_grad = grads_in.reshape(IMAGES, SEQ, D)
    total = jnp.float32(0.0)
    for item in sums:
        total = total + jnp.sum(item * item)
    grad_norm = jnp.sqrt(total)
    scale_clip = jnp.minimum(1.0, CLIP_NORM / (grad_norm + 1e-06))
    qkv_out = adam_step(sums[0], qkv_weight, qkv_first, qkv_second, qkv_average, scale_clip, WEIGHT_DECAY)
    proj_out = adam_step(sums[1], proj_weight, proj_first, proj_second, proj_average, scale_clip, WEIGHT_DECAY)
    up_out = adam_step(sums[2], up_weight, up_first, up_second, up_average, scale_clip, WEIGHT_DECAY)
    down_out = adam_step(sums[3], down_weight, down_first, down_second, down_average, scale_clip, WEIGHT_DECAY)
    head_out = adam_step(sums[4], head_params, head_first, head_second, head_average, scale_clip, 0.0)
    rep_out = adam_step(sums[5], rep_params, rep_first, rep_second, rep_average, scale_clip, 0.0)
    return (block_output, input_grad, grad_norm, qkv_out[0], qkv_out[1], qkv_out[2], qkv_out[3], qkv_out[4], qkv_out[5], proj_out[0], proj_out[1], proj_out[2], proj_out[3], proj_out[4], proj_out[5], up_out[0], up_out[1], up_out[2], up_out[3], up_out[4], up_out[5], down_out[0], down_out[1], down_out[2], down_out[3], down_out[4], down_out[5], head_out[0], head_out[1], head_out[2], head_out[3], head_out[4], head_out[5], rep_out[0], rep_out[1], rep_out[2], rep_out[3], rep_out[4], rep_out[5])
```

```python
from functools import partial

import jax
import jax.numpy as jnp
from jax import lax
from jax.experimental import pallas as pl
from jax.experimental.pallas import tpu as pltpu
from jax.sharding import PartitionSpec as P

HD = 64
GRID = 7
TAPS = 49
STEP = 5
SEQ = 50
LANE = 128
PAD_TOKENS = 64

NORM_EPS = 1e-06
BETA_FIRST = 0.9
BETA_SECOND = 0.999
ADAM_EPS = 1e-08
LEARN_RATE = 0.1
WEIGHT_DECAY = 0.05
CLIP_NORM = 1.0
AVG_KEEP = 0.9
F32 = jnp.float32
BF16 = jnp.bfloat16

NN = (((1,), (0,)), ((), ()))
NT = (((1,), (1,)), ((), ()))
TN = (((0,), (0,)), ((), ()))


def dot(left, right, dims=NN):
    return lax.dot_general(left, right, dims, preferred_element_type=F32)


def rows_at(start, size):
    return pl.ds(pl.multiple_of(start, 16), size)


def norm_parts(values):
    center = values - jnp.mean(values, axis=-1, keepdims=True)
    inv = lax.rsqrt(jnp.mean(center * center, axis=-1, keepdims=True) + NORM_EPS)
    return center * inv, inv


def norm_back(grad, gain, unit, inv):
    scaled = grad * gain
    mean_one = jnp.mean(scaled, axis=-1, keepdims=True)
    mean_two = jnp.mean(scaled * unit, axis=-1, keepdims=True)
    return inv * (scaled - mean_one - unit * mean_two)


def conv_row(src, taps, reach, y, cols, imgs, flip):
    side = 2 * reach + 1
    acc = [None] * GRID
    for a in range(side):
        start = (y + a) * (GRID * imgs)
        vals = [src[rows_at(start + x * imgs, imgs), cols] for x in range(GRID)]
        for b in range(side):
            t = a * side + b
            tap = taps[side * side - 1 - t if flip else t]
            for x in range(GRID):
                other = x + b - reach
                if 0 <= other < GRID:
                    term = tap * vals[other]
                    acc[x] = term if acc[x] is None else acc[x] + term
    return acc


def tap_products(src, grad_row, y, reach, cols, imgs, a, accs):
    side = 2 * reach + 1
    start = (y + a) * (GRID * imgs)
    vals = [src[rows_at(start + x * imgs, imgs), cols] for x in range(GRID)]
    out = []
    for b in range(side):
        acc = accs[b]
        for x in range(GRID):
            other = x + b - reach
            if 0 <= other < GRID:
                acc = acc + grad_row[x] * vals[other]
        out.append(acc)
    return tuple(out)


def pre_kernel(x_ref, og_ref, rp_ref, s0_ref, n1_ref, xp_ref, ogp_ref, ogsum_ref, xs, os):
    imgs, _, width = x_ref.shape
    row = GRID * imgs
    base = row - imgs
    rows = SEQ * imgs
    tiles = width // LANE
    for c in range(tiles):
        cols = slice(c * LANE, (c + 1) * LANE)
        xs[c, 0:row] = jnp.zeros((row, LANE), F32)
        xs[c, 8 * row : 9 * row] = jnp.zeros((row, LANE), F32)
        for i in range(imgs):
            xs[c, pl.ds(base + i, SEQ, stride=imgs), :] = x_ref[i, :, cols].astype(F32)
            os[c, pl.ds(i, SEQ, stride=imgs), :] = og_ref[i, :, cols].astype(F32)
        xp_ref[:, cols] = xs[c, base : base + rows].astype(BF16)
        ogp_ref[:, cols] = os[c].astype(BF16)
        ogsum_ref[:, cols] = jnp.broadcast_to(jnp.sum(os[c], axis=0, keepdims=True), (8, LANE))
        s0_ref[0:imgs, cols] = xs[c, base : base + imgs]
        xs[c, base : base + imgs] = jnp.zeros((imgs, LANE), F32)

    def conv_body(y, carry):
        for c in range(tiles):
            cols = slice(c * LANE, (c + 1) * LANE)
            taps = [rp_ref[t : t + 1, cols] for t in range(9)]
            acc = conv_row(xs.at[c], taps, 1, y, slice(None), imgs, False)
            for x in range(GRID):
                here = xs[c, rows_at((y + 1) * row + x * imgs, imgs)]
                s0_ref[rows_at(imgs + y * row + x * imgs, imgs), cols] = (
                    here + acc[x] + rp_ref[9:10, cols]
                )
        return carry

    lax.fori_loop(0, GRID, conv_body, 0)
    step = 5 * imgs

    def norm_body(r, carry):
        at = rows_at(r * step, step)
        unit, _ = norm_parts(s0_ref[at, :])
        n1_ref[at, :] = (unit * rp_ref[10:11] + rp_ref[11:12]).astype(BF16)
        return carry

    lax.fori_loop(0, rows // step, norm_body, 0)


def head_block_mask(scale):
    row = lax.broadcasted_iota(jnp.int32, (LANE, LANE), 0) // HD
    col = lax.broadcasted_iota(jnp.int32, (LANE, LANE), 1) // HD
    return jnp.where(row == col, F32(scale), F32(0.0))


def joined(refs, cols):
    return jnp.concatenate([ref[0, :, cols] for ref in refs], axis=0)


def attn_kernel(*refs, imgs, nblk):
    _, n1, s0 = refs[:3]
    w = refs[3 : 3 + nblk]
    hp, rp, q_o, k_o, v_o, cv_o, at_o, s1_o, n2_o, qs, ks, vs, fs, vp = refs[3 + nblk :]
    j = pl.program_id(0)
    rows = SEQ * imgs
    grid_row = GRID * imgs
    first = (3 * GRID - 1) * imgs

    @pl.when(j == 0)
    def _():
        for ref in (qs, ks, vs):
            ref[rows:] = jnp.zeros((ref.shape[0] - rows, LANE), F32)
        vp[0:first] = jnp.zeros((first, LANE), F32)
        vp[first + rows :] = jnp.zeros((vp.shape[0] - first - rows, LANE), F32)
        s1_o[...] = s0[...] + rp[14:15]

    wq = joined(w, slice(0, 3 * LANE))
    chunk = 10 * imgs
    for r in range(0, rows, chunk):
        qkv = dot(n1[r : r + chunk], wq)
        q = qkv[:, 0:LANE] + hp[50:51]
        qs[r : r + chunk] = q
        q_o[0, r : r + chunk] = q
        ks[r : r + chunk] = qkv[:, LANE : 2 * LANE]
        v = qkv[:, 2 * LANE :] + hp[51:52]
        vs[r : r + chunk] = v
        v_o[0, r : r + chunk] = v
        vp[first + r : first + r + chunk] = v
    vp[first : first + imgs] = jnp.zeros((imgs, LANE), F32)
    keys = ks[0:rows].reshape(SEQ, imgs, LANE)
    expo = jnp.exp(keys - jnp.max(keys, axis=0, keepdims=True))
    soft = (expo / jnp.sum(expo, axis=0, keepdims=True)).reshape(rows, LANE)
    ks[0:rows] = soft
    k_o[0] = soft
    scale = head_block_mask(HD**-0.5)

    def image_body(i, carry):
        at = pl.ds(i, PAD_TOKENS, stride=imgs)
        ctx = dot(ks[at, :].astype(BF16), vs[at, :].astype(BF16), TN) * scale
        fs[at, :] = dot(qs[at, :].astype(BF16), ctx.astype(BF16))
        return carry

    lax.fori_loop(0, imgs, image_body, 0, unroll=4)
    at_o[0, 0:imgs] = fs[0:imgs].astype(BF16)
    cv_o[0, 0:imgs] = jnp.zeros((imgs, LANE), F32)
    everything = slice(0, LANE)

    def conv_body(y, carry):
        taps = [hp[t : t + 1] for t in range(TAPS)]
        acc = conv_row(vp, taps, 3, y, everything, imgs, False)
        for x in range(GRID):
            at = rows_at(imgs + y * grid_row + x * imgs, imgs)
            value = acc[x] + hp[49:50]
            cv_o[0, at] = value
            at_o[0, at] = (fs[at] + qs[at] * value).astype(BF16)
        return carry

    lax.fori_loop(0, GRID, conv_body, 0)
    s1_o[...] += dot(at_o[0], joined(w, slice(3 * LANE, 4 * LANE)), NT)

    @pl.when(j == pl.num_programs(0) - 1)
    def _():
        step = 5 * imgs

        def norm_body(r, carry):
            at = rows_at(r * step, step)
            unit, _ = norm_parts(s1_o[at, :])
            n2_o[at, :] = (unit * rp[12:13] + rp[13:14]).astype(BF16)
            return carry

        lax.fori_loop(0, rows // step, norm_body, 0)


def mlp_kernel(*refs, imgs, nblk, hid):
    slots, n2, og, s1 = refs[:4]
    w = refs[4 : 4 + nblk]
    ub, rp, out_o, g_o, gal_o, gs1_o, ubg_o, rep_o, hs, ds, hb, gb, oacc, dacc, tile = refs[4 + nblk :]
    j = pl.program_id(0)
    nh = pl.num_programs(0)
    rows = SEQ * imgs
    wu = joined(w, slice(0, hid))
    wd = joined(w, slice(hid, 2 * hid))
    hs[...] = dot(n2[...], wu) + ub[0]
    ds[...] = dot(og[...], wd)
    step = 2 * imgs

    def gelu_body(r, total):
        at = rows_at(r * step, step)
        pre = hs[at, :]
        cdf = 0.5 * (1.0 + lax.erf(pre * F32(0.5**0.5)))
        pdf = jnp.exp(-0.5 * pre * pre) * F32(0.3989422804014327)
        hb[at, :] = (pre * cdf).astype(BF16)
        grad = (ds[at, :] * (cdf + pre * pdf)).astype(BF16)
        gb[at, :] = grad
        wide = grad.astype(F32).reshape(step // 8, 8, hid)
        return total + jnp.sum(wide, axis=0)

    total = lax.fori_loop(0, rows // step, gelu_body, jnp.zeros((8, hid), F32))
    ubg_o[0] = jnp.broadcast_to(jnp.sum(total, axis=0, keepdims=True), (8, hid))
    out_part = dot(hb[...], wd, NT)
    back_part = dot(gb[...], wu, NT)

    @pl.when(j == 0)
    def _():
        oacc[...] = out_part + s1[...] + rp[15:16]
        dacc[...] = back_part

    @pl.when(j > 0)
    def _():
        oacc[...] += out_part
        dacc[...] += back_part

    up = dot(n2[...], gb[...], TN).astype(BF16)
    down = dot(og[...], hb[...], TN).astype(BF16)
    size = up.shape[0] // nblk
    for d in range(nblk):
        at = slots[nblk * nh + d]
        g_o[at, 0, :, 0:hid] = up[d * size : (d + 1) * size]
        g_o[at, 0, :, hid : 2 * hid] = down[d * size : (d + 1) * size]

    @pl.when(j == nh - 1)
    def _():
        width = oacc.shape[1]
        for c in range(width // LANE):
            cols = slice(c * LANE, (c + 1) * LANE)
            tile[...] = oacc[:, cols]
            for i in range(imgs):
                out_o[i, :, cols] = tile[pl.ds(i, SEQ, stride=imgs), :].astype(BF16)
        part = 5 * imgs

        def back_body(r, sums):
            at = rows_at(r * part, part)
            grad = dacc[at, :]
            unit, inv = norm_parts(s1[at, :])
            one = og[at, :].astype(F32) + norm_back(grad, rp[12:13], unit, inv)
            gs1_o[at, :] = one
            low = one.astype(BF16)
            gal_o[at, :] = low

            def fold(v):
                return jnp.sum(v.reshape(part // 8, 8, width), axis=0)

            return (
                sums[0] + fold(grad * unit),
                sums[1] + fold(grad),
                sums[2] + fold(low.astype(F32)),
            )

        zero = jnp.zeros((8, width), F32)
        sums = lax.fori_loop(0, rows // part, back_body, (zero, zero, zero))
        rep_o[...] = jnp.concatenate(
            [jnp.sum(s, axis=0, keepdims=True) for s in sums] + [jnp.zeros((5, width), F32)], axis=0
        )


def attn_back_kernel(*refs, imgs, nblk):
    slots, n1, gal = refs[:3]
    w = refs[3 : 3 + nblk]
    (hp, q_i, k_i, v_i, cv, at_i, g_o, gn1_o, hg_o) = refs[3 + nblk : 12 + nblk]
    qs, ks, vs, gs, fq, fk, fv, vp, gp, gqkv = refs[12 + nblk :]
    j = pl.program_id(0)
    nh = pl.num_programs(0)
    rows = SEQ * imgs
    grid_row = GRID * imgs
    first = (3 * GRID - 1) * imgs

    @pl.when(j == 0)
    def _():
        for ref in (qs, ks, vs, gs):
            ref[rows:] = jnp.zeros((ref.shape[0] - rows, LANE), F32)
        for ref in (vp, gp):
            ref[0:first] = jnp.zeros((first, LANE), F32)
            ref[first + rows :] = jnp.zeros((ref.shape[0] - first - rows, LANE), F32)

    wp = joined(w, slice(3 * LANE, 4 * LANE))
    chunk = 10 * imgs
    for r in range(0, rows, chunk):
        at = slice(r, r + chunk)
        grad = dot(gal[at], wp)
        gs[at] = grad
        q = q_i[0, at]
        v = v_i[0, at]
        qs[at] = q
        ks[at] = k_i[0, at]
        vs[at] = v
        vp[first + r : first + r + chunk] = v
        gp[first + r : first + r + chunk] = grad * q
    vp[first : first + imgs] = jnp.zeros((imgs, LANE), F32)
    gp[first : first + imgs] = jnp.zeros((imgs, LANE), F32)
    scale = head_block_mask(HD**-0.5)

    def image_body(i, carry):
        at = pl.ds(i, PAD_TOKENS, stride=imgs)
        q = qs[at, :].astype(BF16)
        k = ks[at, :].astype(BF16)
        v = vs[at, :].astype(BF16)
        g = gs[at, :].astype(BF16)
        ctx = (dot(k, v, TN) * scale).astype(BF16)
        gctx = (dot(q, g, TN) * scale).astype(BF16)
        fq[at, :] = dot(g, ctx, NT)
        fk[at, :] = dot(v, gctx, NT)
        fv[at, :] = dot(k, gctx)
        return carry

    lax.fori_loop(0, imgs, image_body, 0, unroll=4)
    soft = ks[0:rows].reshape(SEQ, imgs, LANE)
    gsoft = fk[0:rows].reshape(SEQ, imgs, LANE)
    total = jnp.sum(soft * gsoft, axis=0, keepdims=True)
    gqkv[:, LANE : 2 * LANE] = (soft * (gsoft - total)).reshape(rows, LANE).astype(BF16)
    gquery = (fq[0:rows] + gs[0:rows] * cv[0]).astype(BF16)
    gqkv[:, 0:LANE] = gquery
    everything = slice(0, LANE)
    low = fv[0:imgs].astype(BF16)
    gqkv[0:imgs, 2 * LANE :] = low

    def conv_body(y, carry):
        taps = [hp[t : t + 1] for t in range(TAPS)]
        acc = conv_row(gp, taps, 3, y, everything, imgs, True)
        for x in range(GRID):
            at = rows_at(imgs + y * grid_row + x * imgs, imgs)
            value = (fv[at] + acc[x]).astype(BF16)
            gqkv[at, 2 * LANE :] = value
            carry = carry + value.astype(F32)
        return carry

    value_sum = lax.fori_loop(0, GRID, conv_body, low.astype(F32))
    side = GRID
    zero = jnp.zeros((imgs, LANE), F32)
    for a in range(side):

        def tap_body(y, accs, a=a):
            start = (y + 3) * grid_row
            grad_row = [gp[rows_at(start + x * imgs, imgs)] for x in range(GRID)]
            return tap_products(vp, grad_row, y, 3, everything, imgs, a, accs)

        accs = lax.fori_loop(0, GRID, tap_body, (zero,) * side)
        hg_o[0, a * side : (a + 1) * side] = jnp.concatenate(
            [jnp.sum(acc, axis=0, keepdims=True) for acc in accs], axis=0
        )
    conv_sum = jnp.sum(gp[first : first + rows], axis=0, keepdims=True)
    query_sum = jnp.sum(gquery.astype(F32), axis=0, keepdims=True)
    hg_o[0, 49:50] = conv_sum
    hg_o[0, 50:51] = query_sum
    hg_o[0, 51:52] = jnp.sum(value_sum, axis=0, keepdims=True)
    hg_o[0, 52:56] = jnp.zeros((4, LANE), F32)
    part = dot(gqkv[...], joined(w, slice(0, 3 * LANE)), NT)

    @pl.when(j == 0)
    def _():
        gn1_o[...] = part

    @pl.when(j > 0)
    def _():
        gn1_o[...] += part

    wide = dot(n1[...], gqkv[...], TN).astype(BF16)
    proj = dot(gal[...], at_i[0], TN).astype(BF16)
    size = wide.shape[0] // nblk
    for d in range(nblk):
        at = slots[nblk * nh + d]
        g_o[at, 0, :, 0 : 3 * LANE] = wide[d * size : (d + 1) * size]
        g_o[at, 0, :, 3 * LANE :] = proj[d * size : (d + 1) * size]


def tail_kernel(s0, gs1, gn1, xp, rp, ig_o, rep_o, gz, xs, res):
    imgs, _, width = ig_o.shape
    row = GRID * imgs
    base = row - imgs
    rows = SEQ * imgs
    part = 5 * imgs
    for ref in (gz, xs):
        ref[0:row] = jnp.zeros((row, width), F32)
        ref[8 * row : 9 * row] = jnp.zeros((row, width), F32)

    def fold(v):
        return jnp.sum(v.reshape(-1, 8, width), axis=0)

    def back_body(r, sums):
        at = rows_at(r * part, part)
        grad = gn1[at, :]
        unit, inv = norm_parts(s0[at, :])
        to = rows_at(base + r * part, part)
        gz[to, :] = gs1[at, :] + norm_back(grad, rp[10:11], unit, inv)
        xs[to, :] = xp[at, :].astype(F32)
        return (sums[0] + fold(grad * unit), sums[1] + fold(grad))

    zero = jnp.zeros((8, width), F32)
    sums = lax.fori_loop(0, rows // part, back_body, (zero, zero))
    for c in range(width // LANE):
        res[c, 0:imgs] = gz[base : base + imgs, c * LANE : (c + 1) * LANE]
    gz[base : base + imgs] = jnp.zeros((imgs, width), F32)
    xs[base : base + imgs] = jnp.zeros((imgs, width), F32)
    rep_o[10:11] = jnp.sum(sums[0], axis=0, keepdims=True)
    rep_o[11:12] = jnp.sum(sums[1], axis=0, keepdims=True)
    rep_o[12:16] = jnp.zeros((4, width), F32)
    rep_o[9:10] = jnp.sum(gz[row : 8 * row], axis=0, keepdims=True)

    def conv_body(y, carry):
        for c in range(0, width, LANE):
            cols = slice(c, c + LANE)
            taps = [rp[t : t + 1, cols] for t in range(9)]
            acc = conv_row(gz, taps, 1, y, cols, imgs, True)
            for x in range(GRID):
                here = gz[rows_at((y + 1) * row + x * imgs, imgs), cols]
                res[c // LANE, rows_at(imgs + y * row + x * imgs, imgs)] = here + acc[x]
        return carry

    lax.fori_loop(0, GRID, conv_body, 0)
    nothing = jnp.zeros((imgs, LANE), F32)
    for c in range(0, width, LANE):
        cols = slice(c, c + LANE)

        def tap_body(y, accs, cols=cols):
            start = (y + 1) * row
            grad_row = [gz[rows_at(start + x * imgs, imgs), cols] for x in range(GRID)]
            out = []
            for a in range(3):
                out.extend(tap_products(xs, grad_row, y, 1, cols, imgs, a, accs[3 * a : 3 * a + 3]))
            return tuple(out)

        accs = lax.fori_loop(0, GRID, tap_body, (nothing,) * 9)
        rep_o[0:9, cols] = jnp.concatenate(
            [jnp.sum(acc, axis=0, keepdims=True) for acc in accs], axis=0
        )
    for i in range(imgs):
        for c in range(0, width, LANE):
            ig_o[i, :, c : c + LANE] = res[c // LANE, pl.ds(i, SEQ, stride=imgs), :].astype(BF16)


def whole(shape):
    return pl.BlockSpec(shape, lambda *_: (0,) * len(shape))


def tap_mask(radius):
    reach = jnp.repeat(radius, HD)
    taps = lax.broadcasted_iota(jnp.int32, (TAPS, reach.shape[0]), 0)
    vertical = jnp.abs(taps // 7 - 3)
    horizontal = jnp.abs(taps % 7 - 3)
    inside = (vertical <= reach[None, :]) & (horizontal <= reach[None, :])
    return inside.astype(F32)


def adam_step(raw, weight, first, second, average, scale_clip, decay):
    grad = raw * scale_clip
    first_new = BETA_FIRST * first + (1.0 - BETA_FIRST) * grad
    second_new = BETA_SECOND * second + (1.0 - BETA_SECOND) * grad * grad
    moment_hat = first_new / (1.0 - BETA_FIRST**STEP)
    second_hat = second_new / (1.0 - BETA_SECOND**STEP)
    weight_new = weight - LEARN_RATE * (
        moment_hat / (jnp.sqrt(second_hat) + ADAM_EPS) + decay * weight
    )
    average_new = AVG_KEEP * average + (1.0 - AVG_KEEP) * weight_new
    return (grad, first_new, second_new, weight_new, weight_new.astype(BF16), average_new)


def square_sum(values):
    return jnp.sum(values * values)


class Ring:
    def __init__(self, nd, nh):
        self.low = 2 if nd % 2 == 0 else 1
        self.nd, self.nh, self.up = nd, nh, nd // self.low
        dp = lax.axis_index("dp")
        self.mine = (dp % self.low, dp // self.low, lax.axis_index("head"))

    def turn(self, value, stage, k):
        if stage == "head":
            return lax.ppermute(value, "head", [(i, (i + k) % self.nh) for i in range(self.nh)])
        low, up = self.low, self.up
        if stage == "up":
            pairs = [(i, (i // low + k) % up * low + i % low) for i in range(self.nd)]
        else:
            pairs = [(i, i // low * low + (i % low + k) % low) for i in range(self.nd)]
        return lax.ppermute(value, "dp", pairs)

    def gather(self, shard):
        for stage, size in (("head", self.nh), ("up", self.up), ("low", self.low)):
            shard = jnp.stack([shard] + [self.turn(shard, stage, k) for k in range(1, size)])
        return shard.reshape(self.nd * self.nh, *shard.shape[3:])

    def scatter_sum(self, parts):
        for stage, size in (("low", self.low), ("up", self.up), ("head", self.nh)):
            total = parts[0].astype(F32)
            for k in range(1, size):
                total = total + self.turn(parts[k], stage, k).astype(F32)
            parts = total.astype(parts.dtype) if stage != "head" else total
        return parts

    def gather_slot(self, dp, head):
        low, up, z = self.mine
        back = (low - dp % self.low) % self.low, (up - dp // self.low) % self.up
        return (back[0] * self.up + back[1]) * self.nh + (z - head) % self.nh

    def scatter_slot(self, dp, head):
        low, up, z = self.mine
        on = (dp % self.low - low) % self.low, (dp // self.low - up) % self.up
        return on[0] * self.up + on[1], (head - z) % self.nh


def per_device(
    block_input,
    out_grad,
    kernel_radius,
    qkv_weight,
    qkv_first,
    qkv_second,
    qkv_average,
    proj_weight,
    proj_first,
    proj_second,
    proj_average,
    up_weight,
    up_first,
    up_second,
    up_average,
    down_weight,
    down_first,
    down_second,
    down_average,
    head_params,
    head_first,
    head_second,
    head_average,
    rep_params,
    rep_first,
    rep_second,
    rep_average,
):
    nd, nh = lax.axis_size("dp"), lax.axis_size("head")
    imgs, _, width = block_input.shape
    rows = SEQ * imgs
    span = qkv_weight.shape[0]
    hid = up_weight.shape[1]
    ring = Ring(nd, nh)
    staged = span % 16 == 0

    pack_one = jnp.concatenate(
        [qkv_weight.astype(BF16).reshape(span, 3 * LANE), proj_weight.astype(BF16)], axis=1
    )
    pack_two = jnp.concatenate([up_weight.astype(BF16), down_weight.astype(BF16)], axis=1)
    nblk = nd if staged else 8
    size = width // nblk
    dps = jnp.arange(nblk, dtype=jnp.int32)
    heads = jnp.arange(nh, dtype=jnp.int32)
    if staged:
        gathered_one = ring.gather(pack_one)
        gathered_two = ring.gather(pack_two)
        in_slots = ring.gather_slot(dps[:, None], heads[None, :]).reshape(-1)
        out_rows, _ = ring.scatter_slot(dps, 0)
        _, out_heads = ring.scatter_slot(0, heads)
    else:

        def spread(pack):
            full = lax.all_gather(pack, ("dp", "head"), axis=0)
            full = full.reshape(nd, nh, span, -1).swapaxes(0, 1)
            full = full.reshape(nh, nblk, size, -1).swapaxes(0, 1)
            return full.reshape(nblk * nh, size, -1)

        gathered_one, gathered_two = spread(pack_one), spread(pack_two)
        in_slots = jnp.arange(nblk * nh, dtype=jnp.int32)
        out_rows, out_heads = dps, heads
    slots = jnp.concatenate([in_slots, out_rows, out_heads]).astype(jnp.int32)

    def weight_specs(cols):
        return [
            pl.BlockSpec((1, size, cols), lambda j, s, d=d: (s[d * nh + j], 0, 0))
            for d in range(nblk)
        ]

    grad_spec = lambda cols: pl.BlockSpec(
        (nblk, 1, size, cols), lambda j, s: (0, s[nblk * nh + nblk + j], 0, 0)
    )
    shape = jax.ShapeDtypeStruct
    params = pltpu.CompilerParams(
        dimension_semantics=("arbitrary",), vmem_limit_bytes=60 * 1024 * 1024
    )

    stream_zero, normed_one, pixels, cot, cot_sum = pl.pallas_call(
        pre_kernel,
        out_shape=(
            shape((rows, width), F32),
            shape((rows, width), BF16),
            shape((rows, width), BF16),
            shape((rows, width), BF16),
            shape((8, width), F32),
        ),
        scratch_shapes=[
            pltpu.VMEM((width // LANE, 9 * GRID * imgs, LANE), F32),
            pltpu.VMEM((width // LANE, rows, LANE), F32),
        ],
        compiler_params=pltpu.CompilerParams(vmem_limit_bytes=60 * 1024 * 1024),
        name="pre",
    )(block_input, out_grad, rep_params)

    mask = tap_mask(kernel_radius)
    head_rows = jnp.concatenate([head_params[:TAPS] * mask, head_params[TAPS : TAPS + 7]], axis=0)
    bias_up = head_params[TAPS + 3 :].reshape(nh, 1, hid)
    per_head = shape((nh, rows, LANE), F32)
    tile_spec = pl.BlockSpec((1, rows, LANE), lambda j, s: (j, 0, 0))
    full = whole((rows, width))
    padded = pltpu.VMEM((PAD_TOKENS * imgs, LANE), F32)
    framed = pltpu.VMEM((13 * GRID * imgs, LANE), F32)
    hp_spec = pl.BlockSpec((56, LANE), lambda j, s: (0, j))
    queries, keys_soft, values, conv_val, attended, stream_one, normed_two = pl.pallas_call(
        partial(attn_kernel, imgs=imgs, nblk=nblk),
        out_shape=(
            per_head,
            per_head,
            per_head,
            per_head,
            shape((nh, rows, LANE), BF16),
            shape((rows, width), F32),
            shape((rows, width), BF16),
        ),
        grid_spec=pltpu.PrefetchScalarGridSpec(
            num_scalar_prefetch=1,
            grid=(nh,),
            in_specs=[full, full] + weight_specs(4 * LANE) + [hp_spec, whole((16, width))],
            out_specs=[tile_spec] * 5 + [full, full],
            scratch_shapes=[padded] * 4 + [framed],
        ),
        compiler_params=params,
        name="attn",
    )(slots, normed_one, stream_zero, *[gathered_one] * nblk, head_rows, rep_params)

    output, grad_two, grad_low, grad_one, bias_grad, rep_mid = pl.pallas_call(
        partial(mlp_kernel, imgs=imgs, nblk=nblk, hid=hid),
        out_shape=(
            shape((imgs, SEQ, width), BF16),
            shape((nblk, nh, size, 2 * hid), BF16),
            shape((rows, width), BF16),
            shape((rows, width), F32),
            shape((nh, 8, hid), F32),
            shape((8, width), F32),
        ),
        grid_spec=pltpu.PrefetchScalarGridSpec(
            num_scalar_prefetch=1,
            grid=(nh,),
            in_specs=[full, full, full]
            + weight_specs(2 * hid)
            + [pl.BlockSpec((1, 1, hid), lambda j, s: (j, 0, 0)), whole((16, width))],
            out_specs=[
                whole((imgs, SEQ, width)),
                grad_spec(2 * hid),
                full,
                full,
                pl.BlockSpec((1, 8, hid), lambda j, s: (j, 0, 0)),
                whole((8, width)),
            ],
            scratch_shapes=[
                pltpu.VMEM((rows, hid), F32),
                pltpu.VMEM((rows, hid), F32),
                pltpu.VMEM((rows, hid), BF16),
                pltpu.VMEM((rows, hid), BF16),
                pltpu.VMEM((rows, width), F32),
                pltpu.VMEM((rows, width), F32),
                pltpu.VMEM((rows, LANE), F32),
            ],
        ),
        compiler_params=params,
        name="mlp",
    )(slots, normed_two, cot, stream_one, *[gathered_two] * nblk, bias_up, rep_params)

    grad_w_one, grad_norm_one, head_grad = pl.pallas_call(
        partial(attn_back_kernel, imgs=imgs, nblk=nblk),
        out_shape=(
            shape((nblk, nh, size, 4 * LANE), BF16),
            shape((rows, width), F32),
            shape((nh, 56, LANE), F32),
        ),
        grid_spec=pltpu.PrefetchScalarGridSpec(
            num_scalar_prefetch=1,
            grid=(nh,),
            in_specs=[full, full] + weight_specs(4 * LANE) + [hp_spec] + [tile_spec] * 5,
            out_specs=[
                grad_spec(4 * LANE),
                full,
                pl.BlockSpec((1, 56, LANE), lambda j, s: (j, 0, 0)),
            ],
            scratch_shapes=[padded] * 7 + [framed] * 2 + [pltpu.VMEM((rows, 3 * LANE), BF16)],
        ),
        compiler_params=params,
        name="attn_back",
    )(
        slots,
        normed_one,
        grad_low,
        *[gathered_one] * nblk,
        head_rows,
        queries,
        keys_soft,
        values,
        conv_val,
        attended,
    )

    input_grad, rep_top = pl.pallas_call(
        tail_kernel,
        out_shape=(shape((imgs, SEQ, width), BF16), shape((16, width), F32)),
        scratch_shapes=[
            pltpu.VMEM((9 * GRID * imgs, width), F32),
            pltpu.VMEM((9 * GRID * imgs, width), F32),
            pltpu.VMEM((width // LANE, rows, LANE), F32),
        ],
        compiler_params=pltpu.CompilerParams(vmem_limit_bytes=60 * 1024 * 1024),
        name="tail",
    )(stream_zero, grad_one, grad_norm_one, pixels, rep_params)

    rep_grad = jnp.concatenate([rep_top[:12], rep_mid[:3], cot_sum[:1]], axis=0)
    head_part = head_grad.transpose(1, 0, 2).reshape(56, width)
    head_part = jnp.concatenate(
        [head_part[:TAPS] * mask, head_part[TAPS : TAPS + 3], bias_grad[:, 0].reshape(-1, width)],
        axis=0,
    )
    small = jnp.concatenate([head_part, rep_grad], axis=0)
    head_count = head_part.shape[0]
    if staged:
        two = ring.scatter_sum(grad_two.reshape(ring.low, ring.up, nh, size, -1))
        one = ring.scatter_sum(grad_w_one.reshape(ring.low, ring.up, nh, size, -1))
        ndev = nd * nh
        cells = small.size // ndev
        order = jnp.arange(ndev, dtype=jnp.int32)
        low, up, z = ring.mine
        own = (
            ((order // (ring.up * nh) + low) % ring.low)
            + ((order // nh + up) % ring.up) * ring.low
        ) * nh + (order + z) % nh
        turned = jnp.take(small.reshape(ndev, cells), own, axis=0)
        share = ring.scatter_sum(turned.reshape(ring.low, ring.up, nh, cells // LANE, LANE))
        partial_sum = square_sum(one) + square_sum(two)
        tail = jnp.zeros((1, LANE), F32) + partial_sum
        everyone = ring.gather(jnp.concatenate([share, tail], axis=0))
        mat_total = jnp.sum(everyone[:, -1, 0])
        back = ring.gather_slot(order // nh, order % nh)
        small_sum = jnp.take(everyone[:, :-1].reshape(ndev, cells), back, axis=0)
        small_sum = small_sum.reshape(small.shape)
    else:

        def owned(grads):
            full = grads.swapaxes(0, 1).reshape(nh, nd, span, -1).swapaxes(0, 1)
            full = full.reshape(nd * nh, span, -1)
            return lax.psum_scatter(
                full, ("dp", "head"), scatter_dimension=0, tiled=False
            ).astype(F32)

        one, two = owned(grad_w_one), owned(grad_two)
        small_sum, mat_total = lax.psum(
            (small, square_sum(one) + square_sum(two)), ("dp", "head")
        )
    head_sum, rep_sum = small_sum[:head_count], small_sum[head_count:]
    qkv_raw = one[:, : 3 * LANE].reshape(qkv_weight.shape)
    proj_raw = one[:, 3 * LANE :]
    up_raw = two[:, :hid]
    down_raw = two[:, hid:]
    total = mat_total + square_sum(small_sum)
    grad_norm = jnp.sqrt(total)
    scale_clip = jnp.minimum(1.0, CLIP_NORM / (grad_norm + 1e-06))
    qkv_out = adam_step(
        qkv_raw, qkv_weight, qkv_first, qkv_second, qkv_average, scale_clip, WEIGHT_DECAY
    )
    proj_out = adam_step(
        proj_raw, proj_weight, proj_first, proj_second, proj_average, scale_clip, WEIGHT_DECAY
    )
    up_out = adam_step(up_raw, up_weight, up_first, up_second, up_average, scale_clip, WEIGHT_DECAY)
    down_out = adam_step(
        down_raw, down_weight, down_first, down_second, down_average, scale_clip, WEIGHT_DECAY
    )
    head_out = adam_step(
        head_sum, head_params, head_first, head_second, head_average, scale_clip, 0.0
    )
    rep_out = adam_step(rep_sum, rep_params, rep_first, rep_second, rep_average, scale_clip, 0.0)
    return (
        output,
        input_grad,
        grad_norm,
        *qkv_out,
        *proj_out,
        *up_out,
        *down_out,
        *head_out,
        *rep_out,
    )


def solution(mesh):
    tokens = P(("dp", "head"), None, None)
    qkv = P("dp", None, "head")
    mat = P("dp", "head")
    in_specs = (tokens, tokens, P()) + (qkv,) * 4 + (mat,) * 12 + (P(),) * 8
    out_specs = (tokens, tokens, P()) + (qkv,) * 6 + (mat,) * 18 + (P(),) * 12
    return jax.shard_map(
        per_device, mesh=mesh, in_specs=in_specs, out_specs=out_specs, check_vma=False
    )
```

```python
from functools import partial

import jax
import jax.numpy as jnp
from jax import lax
from jax.experimental import pallas as pl
from jax.experimental.pallas import tpu as pltpu
from jax.sharding import PartitionSpec as P


HD = 64
GRID = 7
TAPS = 49
STEP = 5
SEQ = 50
LANE = 128
PAD_TOKENS = 64

NORM_EPS = 1e-06
BETA_FIRST = 0.9
BETA_SECOND = 0.999
ADAM_EPS = 1e-08
LEARN_RATE = 0.1
WEIGHT_DECAY = 0.05
CLIP_NORM = 1.0
AVG_KEEP = 0.9

F32 = jnp.float32
BF16 = jnp.bfloat16

NN = (((1,), (0,)), ((), ()))
NT = (((1,), (1,)), ((), ()))
TN = (((0,), (0,)), ((), ()))


def dot(left, right, dims=NN):
    return lax.dot_general(left, right, dims, preferred_element_type=F32)


def rows_at(start, size):
    return pl.ds(pl.multiple_of(start, 16), size)


def norm_parts(values):
    center = values - jnp.mean(values, axis=-1, keepdims=True)
    inv = lax.rsqrt(jnp.mean(center * center, axis=-1, keepdims=True) + NORM_EPS)
    return center * inv, inv


def norm_back(grad, gain, unit, inv):
    scaled = grad * gain
    mean_one = jnp.mean(scaled, axis=-1, keepdims=True)
    mean_two = jnp.mean(scaled * unit, axis=-1, keepdims=True)
    return inv * (scaled - mean_one - unit * mean_two)


def conv_row(src, taps, reach, y, cols, imgs, flip):
    side = 2 * reach + 1
    acc = [None] * GRID
    for a in range(side):
        start = (y + a) * (GRID * imgs)
        vals = [src[rows_at(start + x * imgs, imgs), cols] for x in range(GRID)]
        for b in range(side):
            t = a * side + b
            tap = taps[side * side - 1 - t if flip else t]
            for x in range(GRID):
                other = x + b - reach
                if 0 <= other < GRID:
                    term = tap * vals[other]
                    acc[x] = term if acc[x] is None else acc[x] + term
    return acc


def tap_products(src, grad_row, y, reach, cols, imgs, a, accs):
    side = 2 * reach + 1
    start = (y + a) * (GRID * imgs)
    vals = [src[rows_at(start + x * imgs, imgs), cols] for x in range(GRID)]
    out = []
    for b in range(side):
        acc = accs[b]
        for x in range(GRID):
            other = x + b - reach
            if 0 <= other < GRID:
                acc = acc + grad_row[x] * vals[other]
        out.append(acc)
    return tuple(out)


def transposed(out, src, rows):
    for r in range(0, rows, LANE):
        stop = min(r + LANE, rows)
        out[:, r:stop] = src[r:stop].T


def pre_kernel(x_ref, og_ref, rp_ref, s0_ref, n1_ref, n1t_ref, ogt_ref, ogsum_ref, xs, *, imgs):
    rows, width = x_ref.shape
    row = GRID * imgs
    base = row - imgs
    xs[0:base] = jnp.zeros((base, width), F32)
    xs[8 * row : 9 * row] = jnp.zeros((row, width), F32)
    xs[base : base + rows] = x_ref[...].astype(F32)
    s0_ref[0:imgs] = xs[base:row]
    xs[base:row] = jnp.zeros((imgs, width), F32)

    def conv_body(y, carry):
        for c in range(0, width, LANE):
            cols = slice(c, c + LANE)
            taps = [rp_ref[t : t + 1, cols] for t in range(9)]
            acc = conv_row(xs, taps, 1, y, cols, imgs, False)
            for x in range(GRID):
                here = xs[rows_at((y + 1) * row + x * imgs, imgs), cols]
                s0_ref[rows_at(imgs + y * row + x * imgs, imgs), cols] = (
                    here + acc[x] + rp_ref[9:10, cols]
                )
        return carry

    lax.fori_loop(0, GRID, conv_body, 0)
    step = 5 * imgs

    def norm_body(r, total):
        at = rows_at(r * step, step)
        unit, _ = norm_parts(s0_ref[at, :])
        n1_ref[at, :] = (unit * rp_ref[10:11] + rp_ref[11:12]).astype(BF16)
        wide = og_ref[at, :].astype(F32).reshape(step // 8, 8, width)
        return total + jnp.sum(wide, axis=0)

    total = lax.fori_loop(0, rows // step, norm_body, jnp.zeros((8, width), F32))
    ogsum_ref[...] = jnp.broadcast_to(jnp.sum(total, axis=0, keepdims=True), (8, width))
    transposed(n1t_ref, n1_ref, rows)
    transposed(ogt_ref, og_ref, rows)


def head_block_mask(scale):
    row = lax.broadcasted_iota(jnp.int32, (LANE, LANE), 0) // HD
    col = lax.broadcasted_iota(jnp.int32, (LANE, LANE), 1) // HD
    return jnp.where(row == col, F32(scale), F32(0.0))


class Slots:
    def __init__(self, up, nh):
        self.up_in, self.up_out = 0, up
        self.head_in = 2 * up
        self.head_col = 2 * up + nh
        self.head_out = 2 * up + 2 * nh
        self.head_abs = 2 * up + 3 * nh
        self.low = 2 * up + 4 * nh
        self.up, self.nh = up, nh


def gather_weights(table, slots, own, recv, to, kinds, width):
    size = own.shape[3]
    for u in range(slots.up):
        at = table[slots.up_in + u]
        for low, src in ((table[slots.low], own), (1 - table[slots.low], recv)):
            rows = rows_at((2 * u + low) * size, size)
            for k in range(kinds):
                to[rows, k * width : (k + 1) * width] = src[at, 0, k]


def scatter_grads(table, slots, left, right, keep, send, kinds, width):
    size = keep.shape[3]
    for low, to in ((table[slots.low], keep), (1 - table[slots.low], send)):
        lhs = [left[rows_at((2 * u + low) * size, size), :] for u in range(slots.up)]
        value = dot(jnp.concatenate(lhs, axis=0), right).astype(BF16)
        for u in range(slots.up):
            at = table[slots.up_out + u]
            for i, k in enumerate(kinds):
                to[at, 0, k] = value[u * size : (u + 1) * size, i * width : (i + 1) * width]


def attn_kernel(
    table, n1, s0, own, recv, hp, rp,
    q_o, k_o, v_o, cv_o, at_o, s1_o, n2_o, n2t_o,
    wbuf, qs, ks, vs, fs, vp,
    *, imgs, slots,
):
    j = pl.program_id(0)
    rows = SEQ * imgs
    grid_row = GRID * imgs
    first = (3 * GRID - 1) * imgs

    @pl.when(j == 0)
    def _():
        for ref in (qs, ks, vs):
            ref[rows:] = jnp.zeros((ref.shape[0] - rows, LANE), F32)
        vp[0:first] = jnp.zeros((first, LANE), F32)
        vp[first + rows :] = jnp.zeros((vp.shape[0] - first - rows, LANE), F32)
        s1_o[...] = s0[...] + rp[14:15]

    gather_weights(table, slots, own, recv, wbuf, 4, LANE)
    chunk = 10 * imgs
    for r in range(0, rows, chunk):
        qkv = dot(n1[r : r + chunk], wbuf[:, 0 : 3 * LANE])
        q = qkv[:, 0:LANE] + hp[50:51]
        qs[r : r + chunk] = q
        q_o[0, r : r + chunk] = q
        ks[r : r + chunk] = qkv[:, LANE : 2 * LANE]
        v = qkv[:, 2 * LANE :] + hp[51:52]
        vs[r : r + chunk] = v
        v_o[0, r : r + chunk] = v
        vp[first + r : first + r + chunk] = v
    vp[first : first + imgs] = jnp.zeros((imgs, LANE), F32)
    keys = ks[0:rows].reshape(SEQ, imgs, LANE)
    expo = jnp.exp(keys - jnp.max(keys, axis=0, keepdims=True))
    soft = (expo / jnp.sum(expo, axis=0, keepdims=True)).reshape(rows, LANE)
    ks[0:rows] = soft
    k_o[0] = soft
    scale = head_block_mask(HD**-0.5)

    def image_body(i, carry):
        at = pl.ds(i, PAD_TOKENS, stride=imgs)
        ctx = dot(ks[at, :].astype(BF16), vs[at, :].astype(BF16), TN) * scale
        fs[at, :] = dot(qs[at, :].astype(BF16), ctx.astype(BF16))
        return carry

    lax.fori_loop(0, imgs, image_body, 0, unroll=4)
    at_o[0, 0:imgs] = fs[0:imgs].astype(BF16)
    cv_o[0, 0:imgs] = jnp.zeros((imgs, LANE), F32)
    everything = slice(0, LANE)

    def conv_body(y, carry):
        taps = [hp[t : t + 1] for t in range(TAPS)]
        acc = conv_row(vp, taps, 3, y, everything, imgs, False)
        for x in range(GRID):
            at = rows_at(imgs + y * grid_row + x * imgs, imgs)
            value = acc[x] + hp[49:50]
            cv_o[0, at] = value
            at_o[0, at] = (fs[at] + qs[at] * value).astype(BF16)
        return carry

    lax.fori_loop(0, GRID, conv_body, 0)
    s1_o[...] += dot(at_o[0], wbuf[:, 3 * LANE :], NT)

    @pl.when(j == pl.num_programs(0) - 1)
    def _():
        step = 5 * imgs

        def norm_body(r, carry):
            at = rows_at(r * step, step)
            unit, _ = norm_parts(s1_o[at, :])
            n2_o[at, :] = (unit * rp[12:13] + rp[13:14]).astype(BF16)
            return carry

        lax.fori_loop(0, rows // step, norm_body, 0)
        transposed(n2t_o, n2_o, rows)


def mlp_kernel(
    table, n2, n2t, og, ogt, s1, own, recv, ub, rp,
    out_o, gn2_o, keep_o, send_o, ubg_o,
    wbuf, hs, ds, hb, gb, oacc,
    *, imgs, slots, hid,
):
    j = pl.program_id(0)
    rows = SEQ * imgs
    gather_weights(table, slots, own, recv, wbuf, 2, hid)
    hs[...] = dot(n2[...], wbuf[:, 0:hid]) + ub[0]
    ds[...] = dot(og[...], wbuf[:, hid:])
    step = 2 * imgs

    def gelu_body(r, total):
        at = rows_at(r * step, step)
        pre = hs[at, :]
        cdf = 0.5 * (1.0 + lax.erf(pre * F32(0.5**0.5)))
        pdf = jnp.exp(-0.5 * pre * pre) * F32(0.3989422804014327)
        hb[at, :] = (pre * cdf).astype(BF16)
        grad = (ds[at, :] * (cdf + pre * pdf)).astype(BF16)
        gb[at, :] = grad
        wide = grad.astype(F32).reshape(step // 8, 8, hid)
        return total + jnp.sum(wide, axis=0)

    total = lax.fori_loop(0, rows // step, gelu_body, jnp.zeros((8, hid), F32))
    ubg_o[0] = jnp.broadcast_to(jnp.sum(total, axis=0, keepdims=True), (8, hid))

    @pl.when(j == 0)
    def _():
        oacc[...] = s1[...] + rp[15:16]
        gn2_o[...] = jnp.zeros(gn2_o.shape, F32)

    chunk = 10 * imgs
    for r in range(0, rows, chunk):
        at = slice(r, r + chunk)
        oacc[at] += dot(hb[at], wbuf[:, hid:], NT)
        gn2_o[at] += dot(gb[at], wbuf[:, 0:hid], NT)
    scatter_grads(table, slots, n2t, gb[...], keep_o, send_o, (0,), hid)
    scatter_grads(table, slots, ogt, hb[...], keep_o, send_o, (1,), hid)

    @pl.when(j == pl.num_programs(0) - 1)
    def _():
        out_o[...] = oacc[...].astype(BF16)


def mid_kernel(gn2, s1, og, rp, gs1_o, gal_o, galt_o, rep_o, *, imgs):
    rows, width = s1.shape
    part = 5 * imgs

    def fold(v):
        return jnp.sum(v.reshape(part // 8, 8, width), axis=0)

    def back_body(r, sums):
        at = rows_at(r * part, part)
        grad = gn2[at, :]
        unit, inv = norm_parts(s1[at, :])
        one = og[at, :].astype(F32) + norm_back(grad, rp[12:13], unit, inv)
        gs1_o[at, :] = one
        low = one.astype(BF16)
        gal_o[at, :] = low
        return (
            sums[0] + fold(grad * unit),
            sums[1] + fold(grad),
            sums[2] + fold(low.astype(F32)),
        )

    zero = jnp.zeros((8, width), F32)
    sums = lax.fori_loop(0, rows // part, back_body, (zero, zero, zero))
    rep_o[...] = jnp.concatenate(
        [jnp.sum(s, axis=0, keepdims=True) for s in sums] + [jnp.zeros((5, width), F32)], axis=0
    )
    transposed(galt_o, gal_o, rows)


def attn_back_kernel(*refs, imgs, slots, begin):
    table, n1t, gal, galt, own, recv, hp, q_i, k_i, v_i, cv, at_i = refs[:12]
    refs = refs[12:]
    if begin:
        gn1_i, refs = refs[0], refs[1:]
    keep_o, send_o, gn1_o, hg_o, wbuf, qs, ks, vs, gs, fq, fk, fv, vp, gp, gqkv = refs
    j = pl.program_id(0)
    rows = SEQ * imgs
    grid_row = GRID * imgs
    first = (3 * GRID - 1) * imgs

    @pl.when(j == 0)
    def _():
        for ref in (qs, ks, vs, gs):
            ref[rows:] = jnp.zeros((ref.shape[0] - rows, LANE), F32)
        for ref in (vp, gp):
            ref[0:first] = jnp.zeros((first, LANE), F32)
            ref[first + rows :] = jnp.zeros((ref.shape[0] - first - rows, LANE), F32)
        gn1_o[...] = gn1_i[...] if begin else jnp.zeros(gn1_o.shape, F32)

    gather_weights(table, slots, own, recv, wbuf, 4, LANE)
    chunk = 10 * imgs
    for r in range(0, rows, chunk):
        at = slice(r, r + chunk)
        grad = dot(gal[at], wbuf[:, 3 * LANE :])
        gs[at] = grad
        q = q_i[0, at]
        v = v_i[0, at]
        qs[at] = q
        ks[at] = k_i[0, at]
        vs[at] = v
        vp[first + r : first + r + chunk] = v
        gp[first + r : first + r + chunk] = grad * q
    vp[first : first + imgs] = jnp.zeros((imgs, LANE), F32)
    gp[first : first + imgs] = jnp.zeros((imgs, LANE), F32)
    scale = head_block_mask(HD**-0.5)

    def image_body(i, carry):
        at = pl.ds(i, PAD_TOKENS, stride=imgs)
        q = qs[at, :].astype(BF16)
        k = ks[at, :].astype(BF16)
        v = vs[at, :].astype(BF16)
        g = gs[at, :].astype(BF16)
        ctx = (dot(k, v, TN) * scale).astype(BF16)
        gctx = (dot(q, g, TN) * scale).astype(BF16)
        fq[at, :] = dot(g, ctx, NT)
        fk[at, :] = dot(v, gctx, NT)
        fv[at, :] = dot(k, gctx)
        return carry

    lax.fori_loop(0, imgs, image_body, 0, unroll=4)
    soft = ks[0:rows].reshape(SEQ, imgs, LANE)
    gsoft = fk[0:rows].reshape(SEQ, imgs, LANE)
    total = jnp.sum(soft * gsoft, axis=0, keepdims=True)
    gqkv[:, LANE : 2 * LANE] = (soft * (gsoft - total)).reshape(rows, LANE).astype(BF16)
    gquery = (fq[0:rows] + gs[0:rows] * cv[0]).astype(BF16)
    gqkv[:, 0:LANE] = gquery
    everything = slice(0, LANE)
    low = fv[0:imgs].astype(BF16)
    gqkv[0:imgs, 2 * LANE :] = low

    def conv_body(y, carry):
        taps = [hp[t : t + 1] for t in range(TAPS)]
        acc = conv_row(gp, taps, 3, y, everything, imgs, True)
        for x in range(GRID):
            at = rows_at(imgs + y * grid_row + x * imgs, imgs)
            value = (fv[at] + acc[x]).astype(BF16)
            gqkv[at, 2 * LANE :] = value
            carry = carry + value.astype(F32)
        return carry

    value_sum = lax.fori_loop(0, GRID, conv_body, low.astype(F32))
    side = GRID
    zero = jnp.zeros((imgs, LANE), F32)
    for a in range(side):

        def tap_body(y, accs, a=a):
            start = (y + 3) * grid_row
            grad_row = [gp[rows_at(start + x * imgs, imgs)] for x in range(GRID)]
            return tap_products(vp, grad_row, y, 3, everything, imgs, a, accs)

        accs = lax.fori_loop(max(0, 3 - a), GRID - max(0, a - 3), tap_body, (zero,) * side)
        hg_o[0, a * side : (a + 1) * side] = jnp.concatenate(
            [jnp.sum(acc, axis=0, keepdims=True) for acc in accs], axis=0
        )
    conv_sum = jnp.sum(gp[first : first + rows], axis=0, keepdims=True)
    query_sum = jnp.sum(gquery.astype(F32), axis=0, keepdims=True)
    hg_o[0, 49:50] = conv_sum
    hg_o[0, 50:51] = query_sum
    hg_o[0, 51:52] = jnp.sum(value_sum, axis=0, keepdims=True)
    hg_o[0, 52:56] = jnp.zeros((4, LANE), F32)
    for r in range(0, rows, chunk):
        gn1_o[r : r + chunk] += dot(gqkv[r : r + chunk], wbuf[:, 0 : 3 * LANE], NT)
    scatter_grads(table, slots, n1t, gqkv[...], keep_o, send_o, (0, 1, 2), LANE)
    scatter_grads(table, slots, galt, at_i[0], keep_o, send_o, (3,), LANE)


def tail_kernel(
    table, s0, gs1, gn1, xp, rp, hg_one, hg_two, ubg, rep_mid, cot, mask,
    ig_o, small_o, gz, xs, res, sm, rep,
    *, imgs, slots,
):
    rows, width = s0.shape
    row = GRID * imgs
    base = row - imgs
    part = 5 * imgs
    for ref in (gz, xs):
        ref[0:row] = jnp.zeros((row, width), F32)
        ref[8 * row : 9 * row] = jnp.zeros((row, width), F32)

    def fold(v):
        return jnp.sum(v.reshape(-1, 8, width), axis=0)

    def back_body(r, sums):
        at = rows_at(r * part, part)
        grad = gn1[at, :]
        unit, inv = norm_parts(s0[at, :])
        to = rows_at(base + r * part, part)
        gz[to, :] = gs1[at, :] + norm_back(grad, rp[10:11], unit, inv)
        xs[to, :] = xp[at, :].astype(F32)
        return (sums[0] + fold(grad * unit), sums[1] + fold(grad))

    zero = jnp.zeros((8, width), F32)
    sums = lax.fori_loop(0, rows // part, back_body, (zero, zero))
    res[0:imgs] = gz[base : base + imgs]
    gz[base : base + imgs] = jnp.zeros((imgs, width), F32)
    xs[base : base + imgs] = jnp.zeros((imgs, width), F32)
    rep[9:10] = jnp.sum(gz[row : 8 * row], axis=0, keepdims=True)
    rep[10:11] = jnp.sum(sums[0], axis=0, keepdims=True)
    rep[11:12] = jnp.sum(sums[1], axis=0, keepdims=True)
    rep[12:15] = rep_mid[0:3]
    rep[15:16] = cot[0:1]

    def conv_body(y, carry):
        for c in range(0, width, LANE):
            cols = slice(c, c + LANE)
            taps = [rp[t : t + 1, cols] for t in range(9)]
            acc = conv_row(gz, taps, 1, y, cols, imgs, True)
            for x in range(GRID):
                here = gz[rows_at((y + 1) * row + x * imgs, imgs), cols]
                res[rows_at(imgs + y * row + x * imgs, imgs), cols] = here + acc[x]
        return carry

    lax.fori_loop(0, GRID, conv_body, 0)
    nothing = jnp.zeros((imgs, LANE), F32)
    for c in range(0, width, LANE):
        cols = slice(c, c + LANE)

        def tap_body(y, accs, cols=cols):
            start = (y + 1) * row
            grad_row = [gz[rows_at(start + x * imgs, imgs), cols] for x in range(GRID)]
            out = []
            for a in range(3):
                out.extend(tap_products(xs, grad_row, y, 1, cols, imgs, a, accs[3 * a : 3 * a + 3]))
            return tuple(out)

        accs = lax.fori_loop(0, GRID, tap_body, (nothing,) * 9)
        rep[0:9, cols] = jnp.concatenate(
            [jnp.sum(acc, axis=0, keepdims=True) for acc in accs], axis=0
        )
    ig_o[...] = res[...].astype(BF16)

    sm[:, 72:] = jnp.zeros((sm.shape[0], sm.shape[1] - 72, LANE), F32)
    half = slots.nh // 2
    for k in range(slots.nh):
        at = table[slots.head_col + k]
        sm[at, 0:56] = hg_one[k] if k < half else hg_two[k - half]
    for t in range(width // LANE):
        cols = slice(t * LANE, (t + 1) * LANE)
        sm[t, 0:TAPS] = sm[t, 0:TAPS] * mask[:, cols]
        for r in range(ubg.shape[0]):
            sm[t, 52 + r : 53 + r] = ubg[r, 0:1, cols]
        sm[t, 56:72] = rep[:, cols]
    span = small_o.shape[2]
    for u in range(small_o.shape[0]):
        for t in range(width // LANE):
            at = table[slots.up_out + u]
            to = table[slots.head_out + t]
            small_o[at, to] = sm[t, u * span : (u + 1) * span]


def whole(shape):
    return pl.BlockSpec(shape, lambda *_: (0,) * len(shape))


def tap_mask(radius):
    reach = jnp.repeat(radius, HD)
    taps = lax.broadcasted_iota(jnp.int32, (TAPS, reach.shape[0]), 0)
    vertical = jnp.abs(taps // 7 - 3)
    horizontal = jnp.abs(taps % 7 - 3)
    inside = (vertical <= reach[None, :]) & (horizontal <= reach[None, :])
    return inside.astype(F32)


def adam_store(outs, raw, weight, first, second, average, clip, decay):
    grad = raw * clip
    first_new = BETA_FIRST * first + (1.0 - BETA_FIRST) * grad
    second_new = BETA_SECOND * second + (1.0 - BETA_SECOND) * grad * grad
    moment_hat = first_new / (1.0 - BETA_FIRST**STEP)
    second_hat = second_new / (1.0 - BETA_SECOND**STEP)
    weight_new = weight - LEARN_RATE * (
        moment_hat / (jnp.sqrt(second_hat) + ADAM_EPS) + decay * weight
    )
    outs[0][...] = grad
    outs[1][...] = first_new
    outs[2][...] = second_new
    outs[3][...] = weight_new
    outs[4][...] = weight_new.astype(BF16)
    outs[5][...] = AVG_KEEP * average + (1.0 - AVG_KEEP) * weight_new


def adam_kernel(table, shares, one, two, *refs, slots, span):
    ins, norm_o, outs, sm = refs[:24], refs[24], refs[25:61], refs[61]
    tiles = sm.shape[0]
    total = jnp.zeros((1, 1), F32)
    for u in range(slots.up):
        for t in range(tiles):
            share = shares[table[slots.up_in + u], table[slots.head_abs + t]]
            sm[t, u * span : (u + 1) * span] = share[0:span]
            total = total + jnp.sum(share[0:span] * share[0:span], keepdims=True)
            total = total + share[span : span + 1, 0:1]
    norm = jnp.sqrt(total)
    clip = jnp.minimum(1.0, CLIP_NORM / (norm + 1e-06))
    norm_o[...] = jnp.broadcast_to(norm, norm_o.shape)
    raws = (one[0:3], one[3], two[0], two[1])
    for p, raw in enumerate(raws):
        state = [ref[...] for ref in ins[4 * p : 4 * p + 4]]
        adam_store(outs[6 * p : 6 * p + 6], raw, *state, clip, WEIGHT_DECAY)
    for p, (begin, end) in ((4, (0, 56)), (5, (56, 72))):
        for t in range(tiles):
            cols = slice(t * LANE, (t + 1) * LANE)
            state = [ref[:, cols] for ref in ins[4 * p : 4 * p + 4]]
            to = [ref.at[:, cols] for ref in outs[6 * p : 6 * p + 6]]
            adam_store(to, sm[t, begin:end], *state, clip, 0.0)


def square_sum(values):
    return jnp.sum(values * values)


class Ring:
    def __init__(self, nd, nh):
        self.low = 2 if nd % 2 == 0 else 1
        self.nd, self.nh, self.up = nd, nh, nd // self.low
        dp = lax.axis_index("dp")
        self.mine = (dp % self.low, dp // self.low, lax.axis_index("head"))

    def turn(self, value, stage, k=1):
        axis = "head" if stage == "head" else "dp"
        low, up = self.low, self.up
        if stage == "head":
            pairs = [(i, (i + k) % self.nh) for i in range(self.nh)]
        elif stage == "up":
            pairs = [(i, (i // low + k) % up * low + i % low) for i in range(self.nd)]
        else:
            pairs = [(i, i // low * low + (i % low + k) % low) for i in range(self.nd)]
        return lax.ppermute(value, axis, pairs)

    def gather(self, shard, stage):
        size = self.nh if stage == "head" else self.up
        return jnp.stack([shard] + [self.turn(shard, stage, k) for k in range(1, size)])

    def scatter(self, parts, stage):
        total = parts[0].astype(F32)
        for k in range(1, len(parts)):
            total = total + self.turn(parts[k], stage, k).astype(F32)
        return total

    def swap_sum(self, keep, send):
        return keep.astype(F32) + self.turn(send, "low").astype(F32)


def per_device(
    block_input,
    out_grad,
    kernel_radius,
    qkv_weight,
    qkv_first,
    qkv_second,
    qkv_average,
    proj_weight,
    proj_first,
    proj_second,
    proj_average,
    up_weight,
    up_first,
    up_second,
    up_average,
    down_weight,
    down_first,
    down_second,
    down_average,
    head_params,
    head_first,
    head_second,
    head_average,
    rep_params,
    rep_first,
    rep_second,
    rep_average,
):
    nd, nh = lax.axis_size("dp"), lax.axis_size("head")
    imgs, _, width = block_input.shape
    rows = SEQ * imgs
    span = qkv_weight.shape[0]
    hid = up_weight.shape[1]
    ring = Ring(nd, nh)
    staged = span % 16 == 0 and ring.low == 2
    tiles = width // LANE

    x = block_input.transpose(1, 0, 2).reshape(rows, width)
    cot = out_grad.transpose(1, 0, 2).reshape(rows, width)
    kinds_first = lambda v: v.transpose(1, 0, 2)
    pack_one = jnp.concatenate(
        [kinds_first(qkv_weight).astype(BF16), proj_weight.astype(BF16)[None]], axis=0
    )
    pack_two = jnp.stack([up_weight.astype(BF16), down_weight.astype(BF16)])
    up = ring.up if staged else 4
    slots = Slots(up, nh)
    ups = jnp.arange(up, dtype=jnp.int32)
    heads = jnp.arange(nh, dtype=jnp.int32)
    if staged:
        size = span
        my_low, my_up, z = ring.mine
        parts = [
            (my_up - ups) % up,
            (ups - my_up) % up,
            (nh - heads) % nh,
            (z + heads) % nh,
            (heads - z) % nh,
            (z - heads) % nh,
            my_low[None],
        ]
        gathered_one = ring.gather(ring.gather(pack_one, "head"), "up")
        other_one = ring.turn(gathered_one, "low")
        gathered_two = ring.gather(ring.gather(pack_two, "head"), "up")
        other_two = ring.turn(gathered_two, "low")
    else:
        size = width // (2 * up)
        parts = [ups, ups, heads, heads, heads, heads, jnp.zeros((1,), jnp.int32)]

        def spread(pack):
            kinds = pack.shape[0]
            full = lax.all_gather(pack, ("dp", "head"), axis=0)
            full = full.reshape(nd, nh, kinds, span, -1).transpose(1, 2, 0, 3, 4)
            full = full.reshape(nh, kinds, up, 2, size, -1).transpose(3, 2, 0, 1, 4, 5)
            return full[0], full[1]

        gathered_one, other_one = spread(pack_one)
        gathered_two, other_two = spread(pack_two)
    table = jnp.concatenate([p.astype(jnp.int32) for p in parts])

    shape = jax.ShapeDtypeStruct

    def params(*semantics):
        return pltpu.CompilerParams(
            dimension_semantics=semantics or None, vmem_limit_bytes=60 * 1024 * 1024
        )

    def cost(us):
        return pl.CostEstimate(flops=0, transcendentals=0, bytes_accessed=int(us * 3.0e6))

    def weight_spec(kinds, cols):
        return pl.BlockSpec(
            (up, 1, kinds, size, cols), lambda j, s: (0, s[slots.head_in + j], 0, 0, 0)
        )

    full = whole((rows, width))
    turned = whole((width, rows))
    rp_spec = whole((16, width))
    wide = shape((rows, width), F32)
    low = shape((rows, width), BF16)
    low_turned = shape((width, rows), BF16)

    stream_zero, normed_one, normed_one_t, cot_t, cot_sum = pl.pallas_call(
        partial(pre_kernel, imgs=imgs),
        out_shape=(wide, low, low_turned, low_turned, shape((8, width), F32)),
        scratch_shapes=[pltpu.VMEM((9 * GRID * imgs, width), F32)],
        compiler_params=params(),
        cost_estimate=cost(9),
        name="pre",
    )(x, cot, rep_params)

    mask = tap_mask(kernel_radius)
    head_rows = jnp.concatenate([head_params[:TAPS] * mask, head_params[TAPS : TAPS + 7]], axis=0)
    bias_up = head_params[TAPS + 3 :].reshape(nh, 1, hid)
    per_head = shape((nh, rows, LANE), F32)
    tile_spec = pl.BlockSpec((1, rows, LANE), lambda j, s: (j, 0, 0))
    padded = pltpu.VMEM((PAD_TOKENS * imgs, LANE), F32)
    framed = pltpu.VMEM((13 * GRID * imgs, LANE), F32)
    w_one = pltpu.VMEM((width, 4 * LANE), BF16)
    hp_spec = pl.BlockSpec((56, LANE), lambda j, s: (0, s[slots.head_col + j]))
    queries, keys_soft, values, conv_val, attended, stream_one, normed_two, normed_two_t = (
        pl.pallas_call(
            partial(attn_kernel, imgs=imgs, slots=slots),
            out_shape=(
                per_head,
                per_head,
                per_head,
                per_head,
                shape((nh, rows, LANE), BF16),
                wide,
                low,
                low_turned,
            ),
            grid_spec=pltpu.PrefetchScalarGridSpec(
                num_scalar_prefetch=1,
                grid=(nh,),
                in_specs=[full, full] + [weight_spec(4, LANE)] * 2 + [hp_spec, rp_spec],
                out_specs=[tile_spec] * 5 + [full, full, turned],
                scratch_shapes=[w_one] + [padded] * 4 + [framed],
            ),
            compiler_params=params("arbitrary"),
            cost_estimate=cost(21),
            name="attn",
        )(table, normed_one, stream_zero, gathered_one, other_one, head_rows, rep_params)
    )

    two_grads = shape((up, nh, 2, size, hid), BF16)
    two_spec = pl.BlockSpec((up, 1, 2, size, hid), lambda j, s: (0, j, 0, 0, 0))
    output, grad_norm_two, keep_two, send_two, bias_grad = pl.pallas_call(
        partial(mlp_kernel, imgs=imgs, slots=slots, hid=hid),
        out_shape=(low, wide, two_grads, two_grads, shape((nh, 8, hid), F32)),
        grid_spec=pltpu.PrefetchScalarGridSpec(
            num_scalar_prefetch=1,
            grid=(nh,),
            in_specs=[full, turned, full, turned, full]
            + [weight_spec(2, hid)] * 2
            + [pl.BlockSpec((1, 1, hid), lambda j, s: (s[slots.head_col + j], 0, 0)), rp_spec],
            out_specs=[
                full,
                full,
                two_spec,
                two_spec,
                pl.BlockSpec((1, 8, hid), lambda j, s: (s[slots.head_col + j], 0, 0)),
            ],
            scratch_shapes=[
                pltpu.VMEM((width, 2 * hid), BF16),
                pltpu.VMEM((rows, hid), F32),
                pltpu.VMEM((rows, hid), F32),
                pltpu.VMEM((rows, hid), BF16),
                pltpu.VMEM((rows, hid), BF16),
                pltpu.VMEM((rows, width), F32),
            ],
        ),
        compiler_params=params("arbitrary"),
        cost_estimate=cost(26),
        name="mlp",
    )(
        table,
        normed_two,
        normed_two_t,
        cot,
        cot_t,
        stream_one,
        gathered_two,
        other_two,
        bias_up,
        rep_params,
    )

    grad_one, grad_low, grad_low_t, rep_mid = pl.pallas_call(
        partial(mid_kernel, imgs=imgs),
        out_shape=(wide, low, low_turned, shape((8, width), F32)),
        compiler_params=params(),
        cost_estimate=cost(4),
        name="mid",
    )(grad_norm_two, stream_one, cot, rep_params)

    half = nh // 2
    one_grads = shape((up, half, 4, size, LANE), BF16)
    one_spec = pl.BlockSpec((up, 1, 4, size, LANE), lambda j, s: (0, j, 0, 0, 0))

    def attn_back(begin, so_far):
        def at_head(j, s):
            return (0, s[slots.head_in + begin + j], 0, 0, 0)

        weights = pl.BlockSpec((up, 1, 4, size, LANE), at_head)
        tile = pl.BlockSpec((1, rows, LANE), lambda j, s: (begin + j, 0, 0))
        taps = pl.BlockSpec((56, LANE), lambda j, s: (0, s[slots.head_col + begin + j]))
        return pl.pallas_call(
            partial(attn_back_kernel, imgs=imgs, slots=slots, begin=begin),
            out_shape=(one_grads, one_grads, wide, shape((half, 56, LANE), F32)),
            grid_spec=pltpu.PrefetchScalarGridSpec(
                num_scalar_prefetch=1,
                grid=(half,),
                in_specs=[turned, full, turned, weights, weights, taps]
                + [tile] * 5
                + [full] * len(so_far),
                out_specs=[
                    one_spec,
                    one_spec,
                    full,
                    pl.BlockSpec((1, 56, LANE), lambda j, s: (j, 0, 0)),
                ],
                scratch_shapes=[w_one]
                + [padded] * 7
                + [framed] * 2
                + [pltpu.VMEM((rows, 3 * LANE), BF16)],
            ),
            compiler_params=params("arbitrary"),
            cost_estimate=cost(19),
            name="attn_back_b" if begin else "attn_back_a",
        )(
            table,
            normed_one_t,
            grad_low,
            grad_low_t,
            gathered_one,
            other_one,
            head_rows,
            queries,
            keys_soft,
            values,
            conv_val,
            attended,
            *so_far,
        )

    keep_a, send_a, grad_half, head_a = attn_back(0, ())
    keep_b, send_b, grad_norm_one, head_b = attn_back(half, (grad_half,))

    small_rows = 8 * pl.cdiv(72, 8 * up)
    smem = pl.BlockSpec(memory_space=pltpu.SMEM)
    vmem = pl.BlockSpec(memory_space=pltpu.VMEM)
    input_grad, small = pl.pallas_call(
        partial(tail_kernel, imgs=imgs, slots=slots),
        out_shape=(low, shape((up, tiles, small_rows, LANE), F32)),
        in_specs=[smem] + [vmem] * 11,
        scratch_shapes=[
            pltpu.VMEM((9 * GRID * imgs, width), F32),
            pltpu.VMEM((9 * GRID * imgs, width), F32),
            pltpu.VMEM((rows, width), F32),
            pltpu.VMEM((tiles, up * small_rows, LANE), F32),
            pltpu.VMEM((16, width), F32),
        ],
        compiler_params=params(),
        cost_estimate=cost(9),
        name="tail",
    )(
        table,
        stream_zero,
        grad_one,
        grad_norm_one,
        x,
        rep_params,
        head_a,
        head_b,
        bias_grad,
        rep_mid,
        cot_sum,
        mask,
    )

    if staged:
        two = ring.swap_sum(keep_two, send_two).astype(BF16)
        two = ring.scatter(two, "up").astype(BF16)
        two = ring.scatter(two, "head")
        one_a = ring.swap_sum(keep_a, send_a).astype(BF16)
        one_b = ring.swap_sum(keep_b, send_b).astype(BF16)
        one = ring.scatter(jnp.concatenate([one_a, one_b], axis=1), "up").astype(BF16)
        one = ring.scatter(one, "head")
        share = ring.swap_sum(small, small)
        share = ring.scatter(share, "up")
        share = ring.scatter(share, "head")
        mine = jnp.zeros((8, LANE), F32) + (square_sum(one) + square_sum(two))
        mine = ring.swap_sum(mine, mine)
        shares = jnp.concatenate([share, mine], axis=0)
        shares = ring.gather(ring.gather(shares, "head"), "up")
    else:

        def owned(even, odd):
            full = jnp.stack([even, odd], axis=1)
            kinds = full.shape[3]
            full = full.transpose(2, 3, 0, 1, 4, 5).reshape(nh, kinds, nd, span, -1)
            full = full.transpose(2, 0, 1, 3, 4).reshape(nd * nh, kinds, span, -1)
            return lax.psum_scatter(full, ("dp", "head"), scatter_dimension=0).astype(F32)

        two = owned(keep_two, send_two)
        one = owned(
            jnp.concatenate([keep_a, keep_b], axis=1), jnp.concatenate([send_a, send_b], axis=1)
        )
        small_sum, mat_total = lax.psum(
            (small, square_sum(one) + square_sum(two)), ("dp", "head")
        )
        first_cell = (lax.broadcasted_iota(jnp.int32, (up, tiles, 8, LANE), 0) == 0) & (
            lax.broadcasted_iota(jnp.int32, (up, tiles, 8, LANE), 1) == 0
        )
        mine = jnp.where(first_cell, mat_total, F32(0.0))
        shares = jnp.concatenate([small_sum, mine], axis=2)

    states = (
        *(kinds_first(v) for v in (qkv_weight, qkv_first, qkv_second, qkv_average)),
        *(proj_weight, proj_first, proj_second, proj_average),
        *(up_weight, up_first, up_second, up_average),
        *(down_weight, down_first, down_second, down_average),
        *(head_params, head_first, head_second, head_average),
        *(rep_params, rep_first, rep_second, rep_average),
    )
    results = []
    for p in range(6):
        like = states[4 * p].shape
        results += [shape(like, BF16 if k == 4 else F32) for k in range(6)]
    norm, *outs = pl.pallas_call(
        partial(adam_kernel, slots=slots, span=small_rows),
        out_shape=(shape((8, LANE), F32), *results),
        in_specs=[smem] + [vmem] * 27,
        scratch_shapes=[pltpu.VMEM((tiles, up * small_rows, LANE), F32)],
        compiler_params=params(),
        cost_estimate=cost(4),
        name="adam",
    )(table, shares, one, two, *states)
    outs[0:6] = [kinds_first(v) for v in outs[0:6]]

    def by_image(v):
        return v.reshape(SEQ, imgs, width).transpose(1, 0, 2)

    return (by_image(output), by_image(input_grad), norm[0, 0], *outs)


def solution(mesh):
    tokens = P(("dp", "head"), None, None)
    qkv = P("dp", None, "head")
    mat = P("dp", "head")
    in_specs = (tokens, tokens, P()) + (qkv,) * 4 + (mat,) * 12 + (P(),) * 8
    out_specs = (tokens, tokens, P()) + (qkv,) * 6 + (mat,) * 18 + (P(),) * 12

    return jax.shard_map(
        per_device, mesh=mesh, in_specs=in_specs, out_specs=out_specs, check_vma=False
    )
```

```python
from functools import partial

import jax
import jax.numpy as jnp
from jax import lax
from jax.experimental import pallas as pl
from jax.experimental.pallas import tpu as pltpu
from jax.sharding import PartitionSpec as P


HD = 64
GRID = 7
TAPS = 49
STEP = 5
SEQ = 50
LANE = 128
PAD_TOKENS = 64
COLS = 256

NORM_EPS = 1e-06
BETA_FIRST = 0.9
BETA_SECOND = 0.999
ADAM_EPS = 1e-08
LEARN_RATE = 0.1
WEIGHT_DECAY = 0.05
CLIP_NORM = 1.0
AVG_KEEP = 0.9

F32 = jnp.float32
BF16 = jnp.bfloat16

NN = (((1,), (0,)), ((), ()))
NT = (((1,), (1,)), ((), ()))
TN = (((0,), (0,)), ((), ()))


def dot(left, right, dims=NN):
    return lax.dot_general(left, right, dims, preferred_element_type=F32)


def rows_at(start, size):
    if isinstance(start, int):
        return pl.ds(start, size)
    return pl.ds(pl.multiple_of(start, 16), size)


def norm_parts(values):
    center = values - jnp.mean(values, axis=-1, keepdims=True)
    inv = lax.rsqrt(jnp.mean(center * center, axis=-1, keepdims=True) + NORM_EPS)
    return center * inv, inv


def norm_back(grad, gain, unit, inv):
    scaled = grad * gain
    mean_one = jnp.mean(scaled, axis=-1, keepdims=True)
    mean_two = jnp.mean(scaled * unit, axis=-1, keepdims=True)
    return inv * (scaled - mean_one - unit * mean_two)


def conv_row(src, taps, reach, y, cols, imgs, flip):
    side = 2 * reach + 1
    acc = [None] * GRID
    inside = range(side)
    if isinstance(y, int):
        inside = range(max(0, reach - y), min(side, GRID + reach - y))
    for a in inside:
        start = (y + a) * (GRID * imgs)
        vals = [src[rows_at(start + x * imgs, imgs), cols] for x in range(GRID)]
        for b in range(side):
            t = a * side + b
            tap = taps[side * side - 1 - t if flip else t]
            for x in range(GRID):
                other = x + b - reach
                if 0 <= other < GRID:
                    term = tap * vals[other]
                    acc[x] = term if acc[x] is None else acc[x] + term
    return acc


def tap_products(src, grad_row, y, reach, cols, imgs, a, accs):
    side = 2 * reach + 1
    start = (y + a) * (GRID * imgs)
    vals = [src[rows_at(start + x * imgs, imgs), cols] for x in range(GRID)]
    out = []
    for b in range(side):
        acc = accs[b]
        for x in range(GRID):
            other = x + b - reach
            if 0 <= other < GRID:
                acc = acc + grad_row[x] * vals[other]
        out.append(acc)
    return tuple(out)


def transposed(out, src, rows):
    for r in range(0, rows, LANE):
        stop = min(r + LANE, rows)
        out[:, r:stop] = src[r:stop].T


def pre_kernel(x_ref, rp_ref, s0_ref, n1_ref, n1t_ref, xs, *, imgs):
    rows, width = x_ref.shape
    row = GRID * imgs
    base = row - imgs
    xs[0:base] = jnp.zeros((base, width), F32)
    xs[8 * row : 9 * row] = jnp.zeros((row, width), F32)
    xs[base : base + rows] = x_ref[...].astype(F32)
    s0_ref[0:imgs] = xs[base:row]
    xs[base:row] = jnp.zeros((imgs, width), F32)

    def conv_body(y, carry):
        for c in range(0, width, LANE):
            cols = slice(c, c + LANE)
            taps = [rp_ref[t : t + 1, cols] for t in range(9)]
            acc = conv_row(xs, taps, 1, y, cols, imgs, False)
            for x in range(GRID):
                here = xs[rows_at((y + 1) * row + x * imgs, imgs), cols]
                s0_ref[rows_at(imgs + y * row + x * imgs, imgs), cols] = (
                    here + acc[x] + rp_ref[9:10, cols]
                )
        return carry

    lax.fori_loop(0, GRID, conv_body, 0)
    step = 5 * imgs

    def norm_body(r, carry):
        at = rows_at(r * step, step)
        unit, _ = norm_parts(s0_ref[at, :])
        n1_ref[at, :] = (unit * rp_ref[10:11] + rp_ref[11:12]).astype(BF16)
        return carry

    lax.fori_loop(0, rows // step, norm_body, 0)
    transposed(n1t_ref, n1_ref, rows)


def cot_kernel(og_ref, ogt_ref, ogsum_ref):
    rows, width = og_ref.shape
    wide = og_ref[...].astype(F32).reshape(rows // 8, 8, width)
    total = jnp.sum(jnp.sum(wide, axis=0), axis=0, keepdims=True)
    ogsum_ref[...] = jnp.broadcast_to(total, (8, width))
    transposed(ogt_ref, og_ref, rows)


def head_block_mask(scale):
    row = lax.broadcasted_iota(jnp.int32, (LANE, LANE), 0) // HD
    col = lax.broadcasted_iota(jnp.int32, (LANE, LANE), 1) // HD
    return jnp.where(row == col, F32(scale), F32(0.0))


class Slots:
    def __init__(self, up, nh):
        self.up_in, self.up_out = 0, up
        self.head_in = 2 * up
        self.head_col = 2 * up + nh
        self.head_out = 2 * up + 2 * nh
        self.head_abs = 2 * up + 3 * nh
        self.low = 2 * up + 4 * nh
        self.up, self.nh = up, nh


def gather_weights(table, slots, own, recv, to, kinds, width):
    size = own.shape[3]
    for u in range(slots.up):
        at = table[slots.up_in + u]
        for low, src in ((table[slots.low], own), (1 - table[slots.low], recv)):
            rows = rows_at((2 * u + low) * size, size)
            for k in range(kinds):
                to[rows, k * width : (k + 1) * width] = src[at, 0, k]


def scatter_grads(table, slots, left, right, keep, send, kinds, width):
    size = keep.shape[3]
    lows = (table[slots.low], 1 - table[slots.low])
    starts = [(2 * u + low) * size for low in lows for u in range(slots.up)]
    lhs = jnp.concatenate([left[rows_at(start, size), :] for start in starts], axis=0)
    step = max(1, COLS // width)
    for n in range(0, len(kinds), step):
        some = kinds[n : n + step]
        value = dot(lhs, right[:, n * width : (n + len(some)) * width]).astype(BF16)
        for b in range(2 * slots.up):
            to = (keep, send)[b // slots.up]
            at = table[slots.up_out + b % slots.up]
            for i, k in enumerate(some):
                to[at, 0, k] = value[b * size : (b + 1) * size, i * width : (i + 1) * width]


def attn_kernel(
    table, n1, s0, own, recv, hp, rp,
    q_o, k_o, v_o, cv_o, at_o, s1_o, n2_o, n2t_o,
    wbuf, qs, ks, vs, fs, vp,
    *, imgs, slots,
):
    j = pl.program_id(0)
    rows = SEQ * imgs
    grid_row = GRID * imgs
    first = (3 * GRID - 1) * imgs

    @pl.when(j == 0)
    def _():
        for ref in (qs, ks, vs):
            ref[rows:] = jnp.zeros((ref.shape[0] - rows, LANE), F32)
        vp[0:first] = jnp.zeros((first, LANE), F32)
        vp[first + rows :] = jnp.zeros((vp.shape[0] - first - rows, LANE), F32)
        s1_o[...] = s0[...] + rp[14:15]

    gather_weights(table, slots, own, recv, wbuf, 4, LANE)
    qk = dot(n1[...], wbuf[:, 0 : 2 * LANE])
    q = qk[:, 0:LANE] + hp[50:51]
    qs[0:rows] = q
    q_o[0] = q
    ks[0:rows] = qk[:, LANE:]
    v = dot(n1[...], wbuf[:, 2 * LANE : 3 * LANE]) + hp[51:52]
    vs[0:rows] = v
    v_o[0] = v
    vp[first : first + rows] = v
    vp[first : first + imgs] = jnp.zeros((imgs, LANE), F32)
    keys = ks[0:rows].reshape(SEQ, imgs, LANE)
    expo = jnp.exp(keys - jnp.max(keys, axis=0, keepdims=True))
    soft = (expo / jnp.sum(expo, axis=0, keepdims=True)).reshape(rows, LANE)
    ks[0:rows] = soft
    k_o[0] = soft
    scale = head_block_mask(HD**-0.5)

    def image_body(i, carry):
        at = pl.ds(i, PAD_TOKENS, stride=imgs)
        ctx = dot(ks[at, :].astype(BF16), vs[at, :].astype(BF16), TN) * scale
        fs[at, :] = dot(qs[at, :].astype(BF16), ctx.astype(BF16))
        return carry

    lax.fori_loop(0, imgs, image_body, 0, unroll=4)
    at_o[0, 0:imgs] = fs[0:imgs].astype(BF16)
    cv_o[0, 0:imgs] = jnp.zeros((imgs, LANE), F32)
    everything = slice(0, LANE)

    def conv_body(y, carry):
        taps = [hp[t : t + 1] for t in range(TAPS)]
        acc = conv_row(vp, taps, 3, y, everything, imgs, False)
        for x in range(GRID):
            at = rows_at(imgs + y * grid_row + x * imgs, imgs)
            value = acc[x] + hp[49:50]
            cv_o[0, at] = value
            at_o[0, at] = (fs[at] + qs[at] * value).astype(BF16)
        return carry

    for y in range(GRID):
        conv_body(y, 0)
    for c in range(0, s1_o.shape[1], COLS):
        s1_o[:, c : c + COLS] += dot(at_o[0], wbuf[c : c + COLS, 3 * LANE :], NT)

    @pl.when(j == pl.num_programs(0) - 1)
    def _():
        step = 5 * imgs

        def norm_body(r, carry):
            at = rows_at(r * step, step)
            unit, _ = norm_parts(s1_o[at, :])
            n2_o[at, :] = (unit * rp[12:13] + rp[13:14]).astype(BF16)
            return carry

        lax.fori_loop(0, rows // step, norm_body, 0)
        transposed(n2t_o, n2_o, rows)


def mlp_kernel(
    table, n2, n2t, og, ogt, s1, own, recv, ub, rp,
    out_o, gn2_o, keep_o, send_o, ubg_o,
    wbuf, hs, ds, hb, gb, oacc,
    *, imgs, slots, hid,
):
    j = pl.program_id(0)
    rows = SEQ * imgs
    gather_weights(table, slots, own, recv, wbuf, 2, hid)
    for c in range(0, hid, COLS):
        hs[:, c : c + COLS] = dot(n2[...], wbuf[:, c : c + COLS]) + ub[0, :, c : c + COLS]
        ds[:, c : c + COLS] = dot(og[...], wbuf[:, hid + c : hid + c + COLS])
    step = 2 * imgs

    def gelu_body(r, total):
        at = rows_at(r * step, step)
        pre = hs[at, :]
        cdf = 0.5 * (1.0 + lax.erf(pre * F32(0.5**0.5)))
        pdf = jnp.exp(-0.5 * pre * pre) * F32(0.3989422804014327)
        hb[at, :] = (pre * cdf).astype(BF16)
        grad = (ds[at, :] * (cdf + pre * pdf)).astype(BF16)
        gb[at, :] = grad
        wide = grad.astype(F32).reshape(step // 8, 8, hid)
        return total + jnp.sum(wide, axis=0)

    total = lax.fori_loop(0, rows // step, gelu_body, jnp.zeros((8, hid), F32))
    ubg_o[0] = jnp.broadcast_to(jnp.sum(total, axis=0, keepdims=True), (8, hid))

    @pl.when(j == 0)
    def _():
        oacc[...] = s1[...] + rp[15:16]
        gn2_o[...] = jnp.zeros(gn2_o.shape, F32)

    for c in range(0, oacc.shape[1], COLS):
        cols = slice(c, c + COLS)
        oacc[:, cols] += dot(hb[...], wbuf[cols, hid:], NT)
        gn2_o[:, cols] += dot(gb[...], wbuf[cols, 0:hid], NT)
    scatter_grads(table, slots, n2t, gb, keep_o, send_o, (0,), hid)
    scatter_grads(table, slots, ogt, hb, keep_o, send_o, (1,), hid)

    @pl.when(j == pl.num_programs(0) - 1)
    def _():
        out_o[...] = oacc[...].astype(BF16)


def mid_kernel(gn2, s1, og, rp, gs1_o, gal_o, galt_o, rep_o, *, imgs):
    rows, width = s1.shape
    part = 5 * imgs

    def fold(v):
        return jnp.sum(v.reshape(part // 8, 8, width), axis=0)

    def back_body(r, sums):
        at = rows_at(r * part, part)
        grad = gn2[at, :]
        unit, inv = norm_parts(s1[at, :])
        one = og[at, :].astype(F32) + norm_back(grad, rp[12:13], unit, inv)
        gs1_o[at, :] = one
        low = one.astype(BF16)
        gal_o[at, :] = low
        return (
            sums[0] + fold(grad * unit),
            sums[1] + fold(grad),
            sums[2] + fold(low.astype(F32)),
        )

    zero = jnp.zeros((8, width), F32)
    sums = lax.fori_loop(0, rows // part, back_body, (zero, zero, zero))
    rep_o[...] = jnp.concatenate(
        [jnp.sum(s, axis=0, keepdims=True) for s in sums] + [jnp.zeros((5, width), F32)], axis=0
    )
    transposed(galt_o, gal_o, rows)


def attn_back_kernel(*refs, imgs, slots, begin):
    table, n1t, gal, galt, own, recv, hp, q_i, k_i, v_i, cv, at_i = refs[:12]
    refs = refs[12:]
    if begin:
        gn1_i, refs = refs[0], refs[1:]
    keep_o, send_o, gn1_o, hg_o, wbuf, qs, ks, vs, gs, fq, fk, fv, vp, gp, gqkv = refs
    j = pl.program_id(0)
    rows = SEQ * imgs
    grid_row = GRID * imgs
    first = (3 * GRID - 1) * imgs

    @pl.when(j == 0)
    def _():
        for ref in (qs, ks, vs, gs):
            ref[rows:] = jnp.zeros((ref.shape[0] - rows, LANE), F32)
        for ref in (vp, gp):
            ref[0:first] = jnp.zeros((first, LANE), F32)
            ref[first + rows :] = jnp.zeros((ref.shape[0] - first - rows, LANE), F32)
        gn1_o[...] = gn1_i[...] if begin else jnp.zeros(gn1_o.shape, F32)

    gather_weights(table, slots, own, recv, wbuf, 4, LANE)
    grad = dot(gal[...], wbuf[:, 3 * LANE :])
    gs[0:rows] = grad
    q = q_i[0]
    v = v_i[0]
    qs[0:rows] = q
    ks[0:rows] = k_i[0]
    vs[0:rows] = v
    vp[first : first + rows] = v
    gp[first : first + rows] = grad * q
    vp[first : first + imgs] = jnp.zeros((imgs, LANE), F32)
    gp[first : first + imgs] = jnp.zeros((imgs, LANE), F32)
    scale = head_block_mask(HD**-0.5)

    def image_body(i, carry):
        at = pl.ds(i, PAD_TOKENS, stride=imgs)
        q = qs[at, :].astype(BF16)
        k = ks[at, :].astype(BF16)
        v = vs[at, :].astype(BF16)
        g = gs[at, :].astype(BF16)
        ctx = (dot(k, v, TN) * scale).astype(BF16)
        gctx = (dot(q, g, TN) * scale).astype(BF16)
        fq[at, :] = dot(g, ctx, NT)
        fk[at, :] = dot(v, gctx, NT)
        fv[at, :] = dot(k, gctx)
        return carry

    lax.fori_loop(0, imgs, image_body, 0, unroll=4)
    soft = ks[0:rows].reshape(SEQ, imgs, LANE)
    gsoft = fk[0:rows].reshape(SEQ, imgs, LANE)
    total = jnp.sum(soft * gsoft, axis=0, keepdims=True)
    gqkv[:, LANE : 2 * LANE] = (soft * (gsoft - total)).reshape(rows, LANE).astype(BF16)
    gquery = (fq[0:rows] + gs[0:rows] * cv[0]).astype(BF16)
    gqkv[:, 0:LANE] = gquery
    everything = slice(0, LANE)
    low = fv[0:imgs].astype(BF16)
    gqkv[0:imgs, 2 * LANE :] = low

    def conv_body(y, carry):
        taps = [hp[t : t + 1] for t in range(TAPS)]
        acc = conv_row(gp, taps, 3, y, everything, imgs, True)
        for x in range(GRID):
            at = rows_at(imgs + y * grid_row + x * imgs, imgs)
            value = (fv[at] + acc[x]).astype(BF16)
            gqkv[at, 2 * LANE :] = value
            carry = carry + value.astype(F32)
        return carry

    value_sum = low.astype(F32)
    for y in range(GRID):
        value_sum = conv_body(y, value_sum)
    side = GRID
    zero = jnp.zeros((imgs, LANE), F32)
    for a in range(side):

        def tap_body(y, accs, a=a):
            start = (y + 3) * grid_row
            grad_row = [gp[rows_at(start + x * imgs, imgs)] for x in range(GRID)]
            return tap_products(vp, grad_row, y, 3, everything, imgs, a, accs)

        accs = lax.fori_loop(max(0, 3 - a), GRID - max(0, a - 3), tap_body, (zero,) * side)
        hg_o[0, a * side : (a + 1) * side] = jnp.concatenate(
            [jnp.sum(acc, axis=0, keepdims=True) for acc in accs], axis=0
        )
    conv_sum = jnp.sum(gp[first : first + rows], axis=0, keepdims=True)
    query_sum = jnp.sum(gquery.astype(F32), axis=0, keepdims=True)
    hg_o[0, 49:50] = conv_sum
    hg_o[0, 50:51] = query_sum
    hg_o[0, 51:52] = jnp.sum(value_sum, axis=0, keepdims=True)
    hg_o[0, 52:56] = jnp.zeros((4, LANE), F32)
    for c in range(0, gn1_o.shape[1], COLS):
        cols = slice(c, c + COLS)
        gn1_o[:, cols] += dot(gqkv[...], wbuf[cols, 0 : 3 * LANE], NT)
    scatter_grads(table, slots, n1t, gqkv, keep_o, send_o, (0, 1, 2), LANE)
    scatter_grads(table, slots, galt, at_i.at[0], keep_o, send_o, (3,), LANE)


def tail_kernel(
    table, s0, gs1, gn1, xp, rp, hg_one, hg_two, ubg, rep_mid, cot, mask,
    ig_o, small_o, gz, xs, res, sm, rep,
    *, imgs, slots,
):
    rows, width = s0.shape
    row = GRID * imgs
    base = row - imgs
    part = 5 * imgs
    for ref in (gz, xs):
        ref[0:row] = jnp.zeros((row, width), F32)
        ref[8 * row : 9 * row] = jnp.zeros((row, width), F32)

    def fold(v):
        return jnp.sum(v.reshape(-1, 8, width), axis=0)

    def back_body(r, sums):
        at = rows_at(r * part, part)
        grad = gn1[at, :]
        unit, inv = norm_parts(s0[at, :])
        to = rows_at(base + r * part, part)
        gz[to, :] = gs1[at, :] + norm_back(grad, rp[10:11], unit, inv)
        xs[to, :] = xp[at, :].astype(F32)
        return (sums[0] + fold(grad * unit), sums[1] + fold(grad))

    zero = jnp.zeros((8, width), F32)
    sums = lax.fori_loop(0, rows // part, back_body, (zero, zero))
    res[0:imgs] = gz[base : base + imgs]
    gz[base : base + imgs] = jnp.zeros((imgs, width), F32)
    xs[base : base + imgs] = jnp.zeros((imgs, width), F32)
    rep[9:10] = jnp.sum(gz[row : 8 * row], axis=0, keepdims=True)
    rep[10:11] = jnp.sum(sums[0], axis=0, keepdims=True)
    rep[11:12] = jnp.sum(sums[1], axis=0, keepdims=True)
    rep[12:15] = rep_mid[0:3]
    rep[15:16] = cot[0:1]

    def conv_body(y, carry):
        for c in range(0, width, LANE):
            cols = slice(c, c + LANE)
            taps = [rp[t : t + 1, cols] for t in range(9)]
            acc = conv_row(gz, taps, 1, y, cols, imgs, True)
            for x in range(GRID):
                here = gz[rows_at((y + 1) * row + x * imgs, imgs), cols]
                res[rows_at(imgs + y * row + x * imgs, imgs), cols] = here + acc[x]
        return carry

    lax.fori_loop(0, GRID, conv_body, 0)
    nothing = jnp.zeros((imgs, LANE), F32)
    for c in range(0, width, LANE):
        cols = slice(c, c + LANE)

        def tap_body(y, accs, cols=cols):
            start = (y + 1) * row
            grad_row = [gz[rows_at(start + x * imgs, imgs), cols] for x in range(GRID)]
            out = []
            for a in range(3):
                out.extend(tap_products(xs, grad_row, y, 1, cols, imgs, a, accs[3 * a : 3 * a + 3]))
            return tuple(out)

        accs = lax.fori_loop(0, GRID, tap_body, (nothing,) * 9)
        rep[0:9, cols] = jnp.concatenate(
            [jnp.sum(acc, axis=0, keepdims=True) for acc in accs], axis=0
        )
    ig_o[...] = res[...].astype(BF16)

    sm[:, 72:] = jnp.zeros((sm.shape[0], sm.shape[1] - 72, LANE), F32)
    half = hg_one.shape[0]
    for k in range(slots.nh):
        at = table[slots.head_col + k]
        sm[at, 0:56] = hg_one[k] if k < half else hg_two[k - half]
    for t in range(width // LANE):
        cols = slice(t * LANE, (t + 1) * LANE)
        sm[t, 0:TAPS] = sm[t, 0:TAPS] * mask[:, cols]
        for r in range(ubg.shape[0]):
            sm[t, 52 + r : 53 + r] = ubg[r, 0:1, cols]
        sm[t, 56:72] = rep[:, cols]
    span = small_o.shape[2]
    for u in range(small_o.shape[0]):
        for t in range(width // LANE):
            at = table[slots.up_out + u]
            to = table[slots.head_out + t]
            small_o[at, to] = sm[t, u * span : (u + 1) * span]


def whole(shape):
    return pl.BlockSpec(shape, lambda *_: (0,) * len(shape))


def tap_mask(radius):
    reach = jnp.repeat(radius, HD)
    taps = lax.broadcasted_iota(jnp.int32, (TAPS, reach.shape[0]), 0)
    vertical = jnp.abs(taps // 7 - 3)
    horizontal = jnp.abs(taps % 7 - 3)
    inside = (vertical <= reach[None, :]) & (horizontal <= reach[None, :])
    return inside.astype(F32)


def adam_store(outs, raw, weight, first, second, average, clip, decay):
    grad = raw * clip
    first_new = BETA_FIRST * first + (1.0 - BETA_FIRST) * grad
    second_new = BETA_SECOND * second + (1.0 - BETA_SECOND) * grad * grad
    moment_hat = first_new / (1.0 - BETA_FIRST**STEP)
    second_hat = second_new / (1.0 - BETA_SECOND**STEP)
    weight_new = weight - LEARN_RATE * (
        moment_hat / (jnp.sqrt(second_hat) + ADAM_EPS) + decay * weight
    )
    outs[0][...] = grad
    outs[1][...] = first_new
    outs[2][...] = second_new
    outs[3][...] = weight_new
    outs[4][...] = weight_new.astype(BF16)
    outs[5][...] = AVG_KEEP * average + (1.0 - AVG_KEEP) * weight_new


def adam_kernel(table, shares, one, two, *refs, slots, span):
    ins, norm_o, outs, sm = refs[:24], refs[24], refs[25:61], refs[61]
    tiles = sm.shape[0]
    total = jnp.zeros((1, 1), F32)
    for u in range(slots.up):
        for t in range(tiles):
            share = shares[table[slots.up_in + u], table[slots.head_abs + t]]
            sm[t, u * span : (u + 1) * span] = share[0:span]
            total = total + jnp.sum(share[0:span] * share[0:span], keepdims=True)
            total = total + share[span : span + 1, 0:1]
    norm = jnp.sqrt(total)
    clip = jnp.minimum(1.0, CLIP_NORM / (norm + 1e-06))
    norm_o[...] = norm
    raws = (one[0:3], one[3], two[0], two[1])
    for p, raw in enumerate(raws):
        state = [ref[...] for ref in ins[4 * p : 4 * p + 4]]
        adam_store(outs[6 * p : 6 * p + 6], raw, *state, clip, WEIGHT_DECAY)
    for p, (begin, end) in ((4, (0, 56)), (5, (56, 72))):
        for t in range(tiles):
            cols = slice(t * LANE, (t + 1) * LANE)
            state = [ref[:, cols] for ref in ins[4 * p : 4 * p + 4]]
            to = [ref.at[:, cols] for ref in outs[6 * p : 6 * p + 6]]
            adam_store(to, sm[t, begin:end], *state, clip, 0.0)


def square_sum(values):
    return jnp.sum(values * values)


class Ring:
    def __init__(self, nd, nh):
        self.low = 2 if nd % 2 == 0 else 1
        self.nd, self.nh, self.up = nd, nh, nd // self.low
        dp = lax.axis_index("dp")
        self.mine = (dp % self.low, dp // self.low, lax.axis_index("head"))

    def turn(self, value, stage, k=1):
        axis = "head" if stage == "head" else "dp"
        low, up = self.low, self.up
        if stage == "head":
            pairs = [(i, (i + k) % self.nh) for i in range(self.nh)]
        elif stage == "up":
            pairs = [(i, (i // low + k) % up * low + i % low) for i in range(self.nd)]
        else:
            pairs = [(i, i // low * low + (i % low + k) % low) for i in range(self.nd)]
        return lax.ppermute(value, axis, pairs)

    def gather(self, shard, stage):
        size = self.nh if stage == "head" else self.up
        return jnp.stack([shard] + [self.turn(shard, stage, k) for k in range(1, size)])

    def scatter(self, parts, stage):
        total = parts[0].astype(F32)
        for k in range(1, len(parts)):
            total = total + self.turn(parts[k], stage, k).astype(F32)
        return total

    def swap_sum(self, keep, send):
        return keep.astype(F32) + self.turn(send, "low").astype(F32)


def per_device(
    block_input,
    out_grad,
    kernel_radius,
    qkv_weight,
    qkv_first,
    qkv_second,
    qkv_average,
    proj_weight,
    proj_first,
    proj_second,
    proj_average,
    up_weight,
    up_first,
    up_second,
    up_average,
    down_weight,
    down_first,
    down_second,
    down_average,
    head_params,
    head_first,
    head_second,
    head_average,
    rep_params,
    rep_first,
    rep_second,
    rep_average,
):
    nd, nh = lax.axis_size("dp"), lax.axis_size("head")
    imgs, _, width = block_input.shape
    rows = SEQ * imgs
    span = qkv_weight.shape[0]
    hid = up_weight.shape[1]
    ring = Ring(nd, nh)
    staged = span % 16 == 0 and ring.low == 2
    tiles = width // LANE

    x = block_input.transpose(1, 0, 2).reshape(rows, width)
    cot = out_grad.transpose(1, 0, 2).reshape(rows, width)
    kinds_first = lambda v: v.transpose(1, 0, 2)
    pack_one = jnp.concatenate(
        [kinds_first(qkv_weight).astype(BF16), proj_weight.astype(BF16)[None]], axis=0
    )
    pack_two = jnp.stack([up_weight.astype(BF16), down_weight.astype(BF16)])
    up = ring.up if staged else 4
    slots = Slots(up, nh)
    ups = jnp.arange(up, dtype=jnp.int32)
    heads = jnp.arange(nh, dtype=jnp.int32)
    if staged:
        size = span
        my_low, my_up, z = ring.mine
        parts = [
            (my_up - ups) % up,
            (ups - my_up) % up,
            (nh - heads) % nh,
            (z + heads) % nh,
            (heads - z) % nh,
            (z - heads) % nh,
            my_low[None],
        ]
        gathered_one = ring.gather(ring.gather(pack_one, "head"), "up")
        other_one = ring.turn(gathered_one, "low")
        gathered_two = ring.gather(ring.gather(pack_two, "head"), "up")
        other_two = ring.turn(gathered_two, "low")
    else:
        size = width // (2 * up)
        parts = [ups, ups, heads, heads, heads, heads, jnp.zeros((1,), jnp.int32)]

        def spread(pack):
            kinds = pack.shape[0]
            full = lax.all_gather(pack, ("dp", "head"), axis=0)
            full = full.reshape(nd, nh, kinds, span, -1).transpose(1, 2, 0, 3, 4)
            full = full.reshape(nh, kinds, up, 2, size, -1).transpose(3, 2, 0, 1, 4, 5)
            return full[0], full[1]

        gathered_one, other_one = spread(pack_one)
        gathered_two, other_two = spread(pack_two)
    table = jnp.concatenate([p.astype(jnp.int32) for p in parts])

    shape = jax.ShapeDtypeStruct

    def params(mebibytes, *semantics):
        return pltpu.CompilerParams(
            dimension_semantics=semantics or None, vmem_limit_bytes=mebibytes * 1024 * 1024
        )

    def cost(us):
        return pl.CostEstimate(flops=0, transcendentals=0, bytes_accessed=int(us * 3.0e6))

    def weight_spec(kinds, cols):
        return pl.BlockSpec(
            (up, 1, kinds, size, cols), lambda j, s: (0, s[slots.head_in + j], 0, 0, 0)
        )

    full = whole((rows, width))
    turned = whole((width, rows))
    rp_spec = whole((16, width))
    wide = shape((rows, width), F32)
    low = shape((rows, width), BF16)
    low_turned = shape((width, rows), BF16)

    stream_zero, normed_one, normed_one_t = pl.pallas_call(
        partial(pre_kernel, imgs=imgs),
        out_shape=(wide, low, low_turned),
        scratch_shapes=[pltpu.VMEM((9 * GRID * imgs, width), F32)],
        compiler_params=params(10),
        cost_estimate=cost(9),
        name="pre",
    )(x, rep_params)
    cot_t, cot_sum = pl.pallas_call(
        cot_kernel,
        out_shape=(low_turned, shape((8, width), F32)),
        compiler_params=params(6),
        cost_estimate=cost(2),
        name="cot",
    )(cot)

    mask = tap_mask(kernel_radius)
    head_rows = jnp.concatenate([head_params[:TAPS] * mask, head_params[TAPS : TAPS + 7]], axis=0)
    bias_up = head_params[TAPS + 3 :].reshape(nh, 1, hid)
    per_head = shape((nh, rows, LANE), F32)
    tile_spec = pl.BlockSpec((1, rows, LANE), lambda j, s: (j, 0, 0))
    padded = pltpu.VMEM((PAD_TOKENS * imgs, LANE), F32)
    framed = pltpu.VMEM((13 * GRID * imgs, LANE), F32)
    w_one = pltpu.VMEM((width, 4 * LANE), BF16)
    hp_spec = pl.BlockSpec((56, LANE), lambda j, s: (0, s[slots.head_col + j]))
    queries, keys_soft, values, conv_val, attended, stream_one, normed_two, normed_two_t = (
        pl.pallas_call(
            partial(attn_kernel, imgs=imgs, slots=slots),
            out_shape=(
                per_head,
                per_head,
                per_head,
                per_head,
                shape((nh, rows, LANE), BF16),
                wide,
                low,
                low_turned,
            ),
            grid_spec=pltpu.PrefetchScalarGridSpec(
                num_scalar_prefetch=1,
                grid=(nh,),
                in_specs=[full, full] + [weight_spec(4, LANE)] * 2 + [hp_spec, rp_spec],
                out_specs=[tile_spec] * 5 + [full, full, turned],
                scratch_shapes=[w_one] + [padded] * 4 + [framed],
            ),
            compiler_params=params(19, "arbitrary"),
            cost_estimate=cost(21),
            name="attn",
        )(table, normed_one, stream_zero, gathered_one, other_one, head_rows, rep_params)
    )

    two_grads = shape((up, nh, 2, size, hid), BF16)
    two_spec = pl.BlockSpec((up, 1, 2, size, hid), lambda j, s: (0, j, 0, 0, 0))
    output, grad_norm_two, keep_two, send_two, bias_grad = pl.pallas_call(
        partial(mlp_kernel, imgs=imgs, slots=slots, hid=hid),
        out_shape=(low, wide, two_grads, two_grads, shape((nh, 8, hid), F32)),
        grid_spec=pltpu.PrefetchScalarGridSpec(
            num_scalar_prefetch=1,
            grid=(nh,),
            in_specs=[full, turned, full, turned, full]
            + [weight_spec(2, hid)] * 2
            + [pl.BlockSpec((1, 1, hid), lambda j, s: (s[slots.head_col + j], 0, 0)), rp_spec],
            out_specs=[
                full,
                full,
                two_spec,
                two_spec,
                pl.BlockSpec((1, 8, hid), lambda j, s: (s[slots.head_col + j], 0, 0)),
            ],
            scratch_shapes=[
                pltpu.VMEM((width, 2 * hid), BF16),
                pltpu.VMEM((rows, hid), F32),
                pltpu.VMEM((rows, hid), F32),
                pltpu.VMEM((rows, hid), BF16),
                pltpu.VMEM((rows, hid), BF16),
                pltpu.VMEM((rows, width), F32),
            ],
        ),
        compiler_params=params(26, "arbitrary"),
        cost_estimate=cost(26),
        name="mlp",
    )(
        table,
        normed_two,
        normed_two_t,
        cot,
        cot_t,
        stream_one,
        gathered_two,
        other_two,
        bias_up,
        rep_params,
    )

    grad_one, grad_low, grad_low_t, rep_mid = pl.pallas_call(
        partial(mid_kernel, imgs=imgs),
        out_shape=(wide, low, low_turned, shape((8, width), F32)),
        compiler_params=params(9),
        cost_estimate=cost(4),
        name="mid",
    )(grad_norm_two, stream_one, cot, rep_params)

    cut = nh - 1
    one_spec = pl.BlockSpec((up, 1, 4, size, LANE), lambda j, s: (0, j, 0, 0, 0))

    def attn_back(begin, count, so_far):
        one_grads = shape((up, count, 4, size, LANE), BF16)

        def at_head(j, s):
            return (0, s[slots.head_in + begin + j], 0, 0, 0)

        weights = pl.BlockSpec((up, 1, 4, size, LANE), at_head)
        tile = pl.BlockSpec((1, rows, LANE), lambda j, s: (begin + j, 0, 0))
        taps = pl.BlockSpec((56, LANE), lambda j, s: (0, s[slots.head_col + begin + j]))
        return pl.pallas_call(
            partial(attn_back_kernel, imgs=imgs, slots=slots, begin=begin),
            out_shape=(one_grads, one_grads, wide, shape((count, 56, LANE), F32)),
            grid_spec=pltpu.PrefetchScalarGridSpec(
                num_scalar_prefetch=1,
                grid=(count,),
                in_specs=[turned, full, turned, weights, weights, taps]
                + [tile] * 5
                + [full] * len(so_far),
                out_specs=[
                    one_spec,
                    one_spec,
                    full,
                    pl.BlockSpec((1, 56, LANE), lambda j, s: (j, 0, 0)),
                ],
                scratch_shapes=[w_one]
                + [padded] * 7
                + [framed] * 2
                + [pltpu.VMEM((rows, 3 * LANE), BF16)],
            ),
            compiler_params=params(21, "arbitrary"),
            cost_estimate=cost(7 * count),
            name="attn_back_b" if begin else "attn_back_a",
        )(
            table,
            normed_one_t,
            grad_low,
            grad_low_t,
            gathered_one,
            other_one,
            head_rows,
            queries,
            keys_soft,
            values,
            conv_val,
            attended,
            *so_far,
        )

    keep_a, send_a, grad_part, head_a = attn_back(0, cut, ())
    keep_b, send_b, grad_norm_one, head_b = attn_back(cut, nh - cut, (grad_part,))

    small_rows = 8 * pl.cdiv(72, 8 * up)
    smem = pl.BlockSpec(memory_space=pltpu.SMEM)
    vmem = pl.BlockSpec(memory_space=pltpu.VMEM)
    input_grad, small = pl.pallas_call(
        partial(tail_kernel, imgs=imgs, slots=slots),
        out_shape=(low, shape((up, tiles, small_rows, LANE), F32)),
        in_specs=[smem] + [vmem] * 11,
        scratch_shapes=[
            pltpu.VMEM((9 * GRID * imgs, width), F32),
            pltpu.VMEM((9 * GRID * imgs, width), F32),
            pltpu.VMEM((rows, width), F32),
            pltpu.VMEM((tiles, up * small_rows, LANE), F32),
            pltpu.VMEM((16, width), F32),
        ],
        compiler_params=params(16),
        cost_estimate=cost(9),
        name="tail",
    )(
        table,
        stream_zero,
        grad_one,
        grad_norm_one,
        x,
        rep_params,
        head_a,
        head_b,
        bias_grad,
        rep_mid,
        cot_sum,
        mask,
    )

    if staged:
        two = ring.swap_sum(keep_two, send_two).astype(BF16)
        two = ring.scatter(two, "up").astype(BF16)
        two = ring.scatter(two, "head")
        one_a = ring.swap_sum(keep_a, send_a).astype(BF16)
        one_b = ring.swap_sum(keep_b, send_b).astype(BF16)
        one = ring.scatter(jnp.concatenate([one_a, one_b], axis=1), "up").astype(BF16)
        share = ring.scatter(small, "up").astype(BF16)
        pad = -small_rows % 16
        rider = jnp.concatenate(
            [one.reshape(nh, 4 * size, LANE), jnp.pad(share, ((0, 0), (0, pad), (0, 0)))], axis=1
        )
        rider = ring.scatter(rider, "head")
        one = rider[: 4 * size].reshape(4, size, LANE)
        share = rider[4 * size : 4 * size + small_rows]
        mine = jnp.zeros((8, LANE), F32) + (square_sum(one) + square_sum(two))
        shares = jnp.concatenate([share, mine], axis=0)
        shares = ring.swap_sum(shares, shares)
        shares = ring.gather(ring.gather(shares, "head"), "up")
    else:

        def owned(even, odd):
            full = jnp.stack([even, odd], axis=1)
            kinds = full.shape[3]
            full = full.transpose(2, 3, 0, 1, 4, 5).reshape(nh, kinds, nd, span, -1)
            full = full.transpose(2, 0, 1, 3, 4).reshape(nd * nh, kinds, span, -1)
            return lax.psum_scatter(full, ("dp", "head"), scatter_dimension=0).astype(F32)

        two = owned(keep_two, send_two)
        one = owned(
            jnp.concatenate([keep_a, keep_b], axis=1), jnp.concatenate([send_a, send_b], axis=1)
        )
        small_sum, mat_total = lax.psum(
            (small, square_sum(one) + square_sum(two)), ("dp", "head")
        )
        first_cell = (lax.broadcasted_iota(jnp.int32, (up, tiles, 8, LANE), 0) == 0) & (
            lax.broadcasted_iota(jnp.int32, (up, tiles, 8, LANE), 1) == 0
        )
        mine = jnp.where(first_cell, mat_total, F32(0.0))
        shares = jnp.concatenate([small_sum, mine], axis=2)

    states = (
        *(kinds_first(v) for v in (qkv_weight, qkv_first, qkv_second, qkv_average)),
        *(proj_weight, proj_first, proj_second, proj_average),
        *(up_weight, up_first, up_second, up_average),
        *(down_weight, down_first, down_second, down_average),
        *(head_params, head_first, head_second, head_average),
        *(rep_params, rep_first, rep_second, rep_average),
    )
    results = []
    for p in range(6):
        like = states[4 * p].shape
        results += [shape(like, BF16 if k == 4 else F32) for k in range(6)]
    norm, *outs = pl.pallas_call(
        partial(adam_kernel, slots=slots, span=small_rows),
        out_shape=(shape((1, 1), F32), *results),
        in_specs=[smem] + [vmem] * 27,
        scratch_shapes=[pltpu.VMEM((tiles, up * small_rows, LANE), F32)],
        compiler_params=params(10),
        cost_estimate=cost(4),
        name="adam",
    )(table, shares, one, two, *states)
    outs[0:6] = [kinds_first(v) for v in outs[0:6]]

    def by_image(v):
        return v.reshape(SEQ, imgs, width).transpose(1, 0, 2)

    return (by_image(output), by_image(input_grad), norm.reshape(()), *outs)


def solution(mesh):
    tokens = P(("dp", "head"), None, None)
    qkv = P("dp", None, "head")
    mat = P("dp", "head")
    in_specs = (tokens, tokens, P()) + (qkv,) * 4 + (mat,) * 12 + (P(),) * 8
    out_specs = (tokens, tokens, P()) + (qkv,) * 6 + (mat,) * 18 + (P(),) * 12

    return jax.shard_map(
        per_device, mesh=mesh, in_specs=in_specs, out_specs=out_specs, check_vma=False
    )
```

```python
import math
from functools import partial

import jax
import jax.numpy as jnp
from jax import lax
from jax.experimental import pallas as pl
from jax.experimental.pallas import tpu as pltpu
from jax.sharding import PartitionSpec as P


HD = 64
GRID = 7
TAPS = 49
STEP = 5
SEQ = 50
LANE = 128
PAD_TOKENS = 64
COLS = 256

NORM_EPS = 1e-06
BETA_FIRST = 0.9
BETA_SECOND = 0.999
ADAM_EPS = 1e-08
LEARN_RATE = 0.1
WEIGHT_DECAY = 0.05
CLIP_NORM = 1.0
AVG_KEEP = 0.9

F32 = jnp.float32
BF16 = jnp.bfloat16

NN = (((1,), (0,)), ((), ()))
NT = (((1,), (1,)), ((), ()))
TN = (((0,), (0,)), ((), ()))


def dot(left, right, dims=NN):
    return lax.dot_general(left, right, dims, preferred_element_type=F32)


def rows_at(start, size):
    if isinstance(start, int):
        return pl.ds(start, size)
    return pl.ds(pl.multiple_of(start, 16), size)


def norm_parts(values):
    center = values - jnp.mean(values, axis=-1, keepdims=True)
    inv = lax.rsqrt(jnp.mean(center * center, axis=-1, keepdims=True) + NORM_EPS)
    return center * inv, inv


def norm_back(grad, gain, unit, inv):
    scaled = grad * gain
    mean_one = jnp.mean(scaled, axis=-1, keepdims=True)
    mean_two = jnp.mean(scaled * unit, axis=-1, keepdims=True)
    return inv * (scaled - mean_one - unit * mean_two)


def conv_row(src, taps, reach, y, cols, imgs, flip):
    side = 2 * reach + 1
    acc = [None] * GRID
    inside = range(side)
    if isinstance(y, int):
        inside = range(max(0, reach - y), min(side, GRID + reach - y))
    for a in inside:
        start = (y + a) * (GRID * imgs)
        vals = [src[rows_at(start + x * imgs, imgs), cols] for x in range(GRID)]
        for b in range(side):
            t = a * side + b
            tap = taps[side * side - 1 - t if flip else t]
            for x in range(GRID):
                other = x + b - reach
                if 0 <= other < GRID:
                    term = tap * vals[other]
                    acc[x] = term if acc[x] is None else acc[x] + term
    return acc


def tap_products(src, grad_row, y, reach, cols, imgs, a, accs):
    side = 2 * reach + 1
    start = (y + a) * (GRID * imgs)
    vals = [src[rows_at(start + x * imgs, imgs), cols] for x in range(GRID)]
    out = []
    for b in range(side):
        acc = accs[b]
        for x in range(GRID):
            other = x + b - reach
            if 0 <= other < GRID:
                acc = acc + grad_row[x] * vals[other]
        out.append(acc)
    return tuple(out)


def transposed(out, src, rows):
    for r in range(0, rows, LANE):
        stop = min(r + LANE, rows)
        out[:, r:stop] = src[r:stop].T


def pre_kernel(x_ref, rp_ref, s0_ref, n1_ref, n1t_ref, xs, *, imgs):
    rows, width = x_ref.shape
    row = GRID * imgs
    base = row - imgs
    xs[0:base] = jnp.zeros((base, width), F32)
    xs[8 * row : 9 * row] = jnp.zeros((row, width), F32)
    xs[base : base + rows] = x_ref[...].astype(F32)
    s0_ref[0:imgs] = xs[base:row]
    xs[base:row] = jnp.zeros((imgs, width), F32)

    def conv_body(y, carry):
        for c in range(0, width, LANE):
            cols = slice(c, c + LANE)
            taps = [rp_ref[t : t + 1, cols] for t in range(9)]
            acc = conv_row(xs, taps, 1, y, cols, imgs, False)
            for x in range(GRID):
                here = xs[rows_at((y + 1) * row + x * imgs, imgs), cols]
                s0_ref[rows_at(imgs + y * row + x * imgs, imgs), cols] = (
                    here + acc[x] + rp_ref[9:10, cols]
                )
        return carry

    lax.fori_loop(0, GRID, conv_body, 0)
    step = 5 * imgs

    def norm_body(r, carry):
        at = rows_at(r * step, step)
        unit, _ = norm_parts(s0_ref[at, :])
        n1_ref[at, :] = (unit * rp_ref[10:11] + rp_ref[11:12]).astype(BF16)
        return carry

    lax.fori_loop(0, rows // step, norm_body, 0)
    transposed(n1t_ref, n1_ref, rows)


def taps_kernel(radius, hp, rows_o, mask_o):
    lane = lax.broadcasted_iota(jnp.int32, (1, hp.shape[1]), 1)
    reach = jnp.zeros((1, hp.shape[1]), jnp.int32)
    for h in range(hp.shape[1] // HD):
        inside = (lane >= h * HD) & (lane < (h + 1) * HD)
        reach = reach + jnp.where(inside, radius[h], 0)
    keep = [jnp.where(reach >= m, F32(1.0), F32(0.0)) for m in range(4)]
    for t in range(TAPS):
        row = keep[max(abs(t // GRID - 3), abs(t % GRID - 3))]
        mask_o[t : t + 1] = row
        rows_o[t : t + 1] = hp[t : t + 1] * row
    rows_o[TAPS:] = hp[TAPS:]


def cot_kernel(og_ref, ogt_ref, ogsum_ref):
    rows, width = og_ref.shape
    wide = og_ref[...].astype(F32).reshape(rows // 8, 8, width)
    total = jnp.sum(jnp.sum(wide, axis=0), axis=0, keepdims=True)
    ogsum_ref[...] = jnp.broadcast_to(total, (8, width))
    transposed(ogt_ref, og_ref, rows)


def head_block_mask(scale):
    row = lax.broadcasted_iota(jnp.int32, (LANE, LANE), 0) // HD
    col = lax.broadcasted_iota(jnp.int32, (LANE, LANE), 1) // HD
    return jnp.where(row == col, F32(scale), F32(0.0))


class Slots:
    def __init__(self, up, nh):
        self.up_in, self.up_out = 0, up
        self.head_in = 2 * up
        self.head_col = 2 * up + nh
        self.head_out = 2 * up + 2 * nh
        self.head_abs = 2 * up + 3 * nh
        self.low = 2 * up + 4 * nh
        self.up, self.nh = up, nh


def gather_weights(table, slots, own, recv, to, starts, width):
    size = own.shape[3]
    for u in range(slots.up):
        at = table[slots.up_in + u]
        for low, src in ((table[slots.low], own), (1 - table[slots.low], recv)):
            rows = rows_at((2 * u + low) * size, size)
            for k, start in enumerate(starts):
                to[rows, start : start + width] = src[at, 0, k]


def scatter_grads(table, slots, left, right, keep, send, kinds, width, head=0, sums=None):
    size = keep.shape[3]
    lows = (table[slots.low], 1 - table[slots.low])
    starts = [(2 * u + low) * size for low in lows for u in range(slots.up)]
    lhs = [left[rows_at(start, size), :] for start in starts]
    if sums is not None:
        lhs.append(jnp.ones((16, left.shape[1]), BF16))
    lhs = jnp.concatenate(lhs, axis=0)
    step = max(1, COLS // width)
    for n in range(0, len(kinds), step):
        some = kinds[n : n + step]
        full = dot(lhs, right[:, n * width : (n + len(some)) * width])
        if sums is not None:
            sums[...] = full[2 * slots.up * size : 2 * slots.up * size + 8]
        value = full[: 2 * slots.up * size].astype(BF16)
        for b in range(2 * slots.up):
            to = (keep, send)[b // slots.up]
            at = table[slots.up_out + b % slots.up]
            for i, k in enumerate(some):
                to[at, head, k] = value[b * size : (b + 1) * size, i * width : (i + 1) * width]


def attn_kernel(
    table, n1, s0, own, recv, hp, rp,
    q_o, k_o, v_o, cv_o, at_o, s1_o, n2_o, n2t_o,
    wbuf, qs, ks, vs, fs, vp,
    *, imgs, slots,
):
    j = pl.program_id(0)
    rows = SEQ * imgs
    grid_row = GRID * imgs
    first = (3 * GRID - 1) * imgs

    @pl.when(j == 0)
    def _():
        for ref in (qs, ks, vs):
            ref[rows:] = jnp.zeros((ref.shape[0] - rows, LANE), F32)
        vp[0:first] = jnp.zeros((first, LANE), F32)
        vp[first + rows :] = jnp.zeros((vp.shape[0] - first - rows, LANE), F32)
        s1_o[...] = s0[...] + rp[14:15]

    gather_weights(table, slots, own, recv, wbuf, range(0, 4 * LANE, LANE), LANE)
    qk = dot(n1[...], wbuf[:, 0 : 2 * LANE])
    q = qk[:, 0:LANE] + hp[50:51]
    qs[0:rows] = q
    q_o[0] = q
    ks[0:rows] = qk[:, LANE:]
    v = dot(n1[...], wbuf[:, 2 * LANE : 3 * LANE]) + hp[51:52]
    vs[0:rows] = v
    v_o[0] = v
    vp[first : first + rows] = v
    vp[first : first + imgs] = jnp.zeros((imgs, LANE), F32)
    keys = ks[0:rows].reshape(SEQ, imgs, LANE)
    expo = jnp.exp(keys - jnp.max(keys, axis=0, keepdims=True))
    soft = (expo / jnp.sum(expo, axis=0, keepdims=True)).reshape(rows, LANE)
    ks[0:rows] = soft
    k_o[0] = soft
    scale = head_block_mask(HD**-0.5)

    def image_body(i, carry):
        at = pl.ds(i, PAD_TOKENS, stride=imgs)
        ctx = dot(ks[at, :].astype(BF16), vs[at, :].astype(BF16), TN) * scale
        fs[at, :] = dot(qs[at, :].astype(BF16), ctx.astype(BF16))
        return carry

    lax.fori_loop(0, imgs, image_body, 0, unroll=8)
    at_o[0, 0:imgs] = fs[0:imgs].astype(BF16)
    cv_o[0, 0:imgs] = jnp.zeros((imgs, LANE), F32)
    everything = slice(0, LANE)

    def conv_body(y, carry):
        taps = [hp[t : t + 1] for t in range(TAPS)]
        acc = conv_row(vp, taps, 3, y, everything, imgs, False)
        for x in range(GRID):
            at = rows_at(imgs + y * grid_row + x * imgs, imgs)
            value = acc[x] + hp[49:50]
            cv_o[0, at] = value
            at_o[0, at] = (fs[at] + qs[at] * value).astype(BF16)
        return carry

    for y in range(GRID):
        conv_body(y, 0)
    for c in range(0, s1_o.shape[1], COLS):
        s1_o[:, c : c + COLS] += dot(at_o[0], wbuf[c : c + COLS, 3 * LANE :], NT)

    @pl.when(j == pl.num_programs(0) - 1)
    def _():
        step = 5 * imgs

        def norm_body(r, carry):
            at = rows_at(r * step, step)
            unit, _ = norm_parts(s1_o[at, :])
            n2_o[at, :] = (unit * rp[12:13] + rp[13:14]).astype(BF16)
            return carry

        lax.fori_loop(0, rows // step, norm_body, 0)
        transposed(n2t_o, n2_o, rows)


def mlp_kernel(table, n2, n2t, og, ogt, s1, *refs, imgs, slots, hid, heads):
    weights, (ub, rp) = refs[: 2 * heads], refs[2 * heads : 2 * heads + 2]
    out_o, gn2_o, keep_o, send_o, ubg_o, wbuf, hs, ds, hb, gb, oacc = refs[2 * heads + 2 :]
    j = pl.program_id(0)
    rows = SEQ * imgs
    span = heads * hid
    for h in range(heads):
        starts = (h * hid, span + h * hid)
        gather_weights(table, slots, weights[h], weights[heads + h], wbuf, starts, hid)
    for h in range(heads):
        bias = ub[table[slots.head_col + j * heads + h]]
        for c in range(0, hid, COLS):
            at = slice(h * hid + c, h * hid + c + COLS)
            hs[:, at] = dot(n2[...], wbuf[:, at]) + bias[:, c : c + COLS]
            ds[:, at] = dot(og[...], wbuf[:, span + at.start : span + at.stop])
    step = 2 * imgs

    def gelu_body(r, carry):
        at = rows_at(r * step, step)
        pre = hs[at, :]
        cdf = 0.5 + 0.5 * lax.erf(pre * F32(0.5**0.5))
        pdf = jnp.exp2(pre * pre * F32(-0.5 * math.log2(math.e)) + F32(-0.5 * math.log2(2 * math.pi)))
        hb[at, :] = (pre * cdf).astype(BF16)
        gb[at, :] = (ds[at, :] * (cdf + pre * pdf)).astype(BF16)
        return carry

    lax.fori_loop(0, rows // step, gelu_body, 0)

    @pl.when(j == 0)
    def _():
        oacc[...] = s1[...] + rp[15:16]
        gn2_o[...] = jnp.zeros(gn2_o.shape, F32)

    for c in range(0, oacc.shape[1], COLS):
        cols = slice(c, c + COLS)
        oacc[:, cols] += dot(hb[...], wbuf[cols, span:], NT)
        gn2_o[:, cols] += dot(gb[...], wbuf[cols, 0:span], NT)
    for h in range(heads):
        cols = slice(h * hid, (h + 1) * hid)
        sums = ubg_o.at[table[slots.head_col + j * heads + h]]
        scatter_grads(table, slots, n2t, gb.at[:, cols], keep_o, send_o, (0,), hid, h, sums)
        scatter_grads(table, slots, ogt, hb.at[:, cols], keep_o, send_o, (1,), hid, h)

    @pl.when(j == pl.num_programs(0) - 1)
    def _():
        out_o[...] = oacc[...].astype(BF16)


def mid_kernel(gn2, s1, og, rp, gs1_o, gal_o, galt_o, rep_o, *, imgs):
    rows, width = s1.shape
    part = 5 * imgs

    def fold(v):
        return jnp.sum(v.reshape(part // 8, 8, width), axis=0)

    def back_body(r, sums):
        at = rows_at(r * part, part)
        grad = gn2[at, :]
        unit, inv = norm_parts(s1[at, :])
        one = og[at, :].astype(F32) + norm_back(grad, rp[12:13], unit, inv)
        gs1_o[at, :] = one
        low = one.astype(BF16)
        gal_o[at, :] = low
        return (
            sums[0] + fold(grad * unit),
            sums[1] + fold(grad),
            sums[2] + fold(low.astype(F32)),
        )

    zero = jnp.zeros((8, width), F32)
    sums = lax.fori_loop(0, rows // part, back_body, (zero, zero, zero))
    rep_o[...] = jnp.concatenate(
        [jnp.sum(s, axis=0, keepdims=True) for s in sums] + [jnp.zeros((5, width), F32)], axis=0
    )
    transposed(galt_o, gal_o, rows)


def attn_back_kernel(*refs, imgs, slots, begin):
    table, n1t, gal, galt, own, recv, hp, q_i, k_i, v_i, cv, at_i = refs[:12]
    refs = refs[12:]
    if begin:
        gn1_i, refs = refs[0], refs[1:]
    keep_o, send_o, gn1_o, hg_o, wbuf, qs, ks, vs, gs, fq, fk, fv, vp, gp, gqkv = refs
    j = pl.program_id(0)
    rows = SEQ * imgs
    grid_row = GRID * imgs
    first = (3 * GRID - 1) * imgs

    @pl.when(j == 0)
    def _():
        for ref in (qs, ks, vs, gs):
            ref[rows:] = jnp.zeros((ref.shape[0] - rows, LANE), F32)
        for ref in (vp, gp):
            ref[0:first] = jnp.zeros((first, LANE), F32)
            ref[first + rows :] = jnp.zeros((ref.shape[0] - first - rows, LANE), F32)
        gn1_o[...] = gn1_i[...] if begin else jnp.zeros(gn1_o.shape, F32)

    gather_weights(table, slots, own, recv, wbuf, range(0, 4 * LANE, LANE), LANE)
    grad = dot(gal[...], wbuf[:, 3 * LANE :])
    gs[0:rows] = grad
    q = q_i[0]
    v = v_i[0]
    qs[0:rows] = q
    ks[0:rows] = k_i[0]
    vs[0:rows] = v
    vp[first : first + rows] = v
    gp[first : first + rows] = grad * q
    vp[first : first + imgs] = jnp.zeros((imgs, LANE), F32)
    gp[first : first + imgs] = jnp.zeros((imgs, LANE), F32)
    scale = head_block_mask(HD**-0.5)

    def image_body(i, carry):
        at = pl.ds(i, PAD_TOKENS, stride=imgs)
        q = qs[at, :].astype(BF16)
        k = ks[at, :].astype(BF16)
        v = vs[at, :].astype(BF16)
        g = gs[at, :].astype(BF16)
        ctx = (dot(k, v, TN) * scale).astype(BF16)
        gctx = (dot(q, g, TN) * scale).astype(BF16)
        fq[at, :] = dot(g, ctx, NT)
        fk[at, :] = dot(v, gctx, NT)
        fv[at, :] = dot(k, gctx)
        return carry

    lax.fori_loop(0, imgs, image_body, 0, unroll=8)
    soft = ks[0:rows].reshape(SEQ, imgs, LANE)
    gsoft = fk[0:rows].reshape(SEQ, imgs, LANE)
    total = jnp.sum(soft * gsoft, axis=0, keepdims=True)
    gqkv[:, LANE : 2 * LANE] = (soft * (gsoft - total)).reshape(rows, LANE).astype(BF16)
    gquery = (fq[0:rows] + gs[0:rows] * cv[0]).astype(BF16)
    gqkv[:, 0:LANE] = gquery
    everything = slice(0, LANE)
    low = fv[0:imgs].astype(BF16)
    gqkv[0:imgs, 2 * LANE :] = low

    def conv_body(y, carry):
        taps = [hp[t : t + 1] for t in range(TAPS)]
        acc = conv_row(gp, taps, 3, y, everything, imgs, True)
        for x in range(GRID):
            at = rows_at(imgs + y * grid_row + x * imgs, imgs)
            value = (fv[at] + acc[x]).astype(BF16)
            gqkv[at, 2 * LANE :] = value
            carry = carry + value.astype(F32)
        return carry

    value_sum = low.astype(F32)
    for y in range(GRID):
        value_sum = conv_body(y, value_sum)
    side = GRID
    zero = jnp.zeros((imgs, LANE), F32)
    for a in range(side):

        def tap_body(y, accs, a=a):
            start = (y + 3) * grid_row
            grad_row = [gp[rows_at(start + x * imgs, imgs)] for x in range(GRID)]
            return tap_products(vp, grad_row, y, 3, everything, imgs, a, accs)

        accs = lax.fori_loop(max(0, 3 - a), GRID - max(0, a - 3), tap_body, (zero,) * side)
        hg_o[0, a * side : (a + 1) * side] = jnp.concatenate(
            [jnp.sum(acc, axis=0, keepdims=True) for acc in accs], axis=0
        )
    conv_sum = jnp.sum(gp[first : first + rows], axis=0, keepdims=True)
    query_sum = jnp.sum(gquery.astype(F32), axis=0, keepdims=True)
    hg_o[0, 49:50] = conv_sum
    hg_o[0, 50:51] = query_sum
    hg_o[0, 51:52] = jnp.sum(value_sum, axis=0, keepdims=True)
    hg_o[0, 52:56] = jnp.zeros((4, LANE), F32)
    for c in range(0, gn1_o.shape[1], COLS):
        cols = slice(c, c + COLS)
        gn1_o[:, cols] += dot(gqkv[...], wbuf[cols, 0 : 3 * LANE], NT)
    scatter_grads(table, slots, n1t, gqkv, keep_o, send_o, (0, 1, 2), LANE)
    scatter_grads(table, slots, galt, at_i.at[0], keep_o, send_o, (3,), LANE)


def tail_kernel(
    table, s0, gs1, gn1, xp, rp, hg_one, hg_two, ubg, rep_mid, cot, mask,
    ig_o, small_o, gz, xs, res, sm, rep,
    *, imgs, slots,
):
    rows, width = s0.shape
    row = GRID * imgs
    base = row - imgs
    part = 5 * imgs
    for ref in (gz, xs):
        ref[0:row] = jnp.zeros((row, width), F32)
        ref[8 * row : 9 * row] = jnp.zeros((row, width), F32)

    def fold(v):
        return jnp.sum(v.reshape(-1, 8, width), axis=0)

    def back_body(r, sums):
        at = rows_at(r * part, part)
        grad = gn1[at, :]
        unit, inv = norm_parts(s0[at, :])
        to = rows_at(base + r * part, part)
        gz[to, :] = gs1[at, :] + norm_back(grad, rp[10:11], unit, inv)
        xs[to, :] = xp[at, :].astype(F32)
        return (sums[0] + fold(grad * unit), sums[1] + fold(grad))

    zero = jnp.zeros((8, width), F32)
    sums = lax.fori_loop(0, rows // part, back_body, (zero, zero))
    res[0:imgs] = gz[base : base + imgs]
    gz[base : base + imgs] = jnp.zeros((imgs, width), F32)
    xs[base : base + imgs] = jnp.zeros((imgs, width), F32)
    rep[9:10] = jnp.sum(gz[row : 8 * row], axis=0, keepdims=True)
    rep[10:11] = jnp.sum(sums[0], axis=0, keepdims=True)
    rep[11:12] = jnp.sum(sums[1], axis=0, keepdims=True)
    rep[12:15] = rep_mid[0:3]
    rep[15:16] = cot[0:1]

    def conv_body(y, carry):
        for c in range(0, width, LANE):
            cols = slice(c, c + LANE)
            taps = [rp[t : t + 1, cols] for t in range(9)]
            acc = conv_row(gz, taps, 1, y, cols, imgs, True)
            for x in range(GRID):
                here = gz[rows_at((y + 1) * row + x * imgs, imgs), cols]
                res[rows_at(imgs + y * row + x * imgs, imgs), cols] = here + acc[x]
        return carry

    lax.fori_loop(0, GRID, conv_body, 0)
    nothing = jnp.zeros((imgs, LANE), F32)
    for c in range(0, width, LANE):
        cols = slice(c, c + LANE)

        def tap_body(y, accs, cols=cols):
            start = (y + 1) * row
            grad_row = [gz[rows_at(start + x * imgs, imgs), cols] for x in range(GRID)]
            out = []
            for a in range(3):
                out.extend(tap_products(xs, grad_row, y, 1, cols, imgs, a, accs[3 * a : 3 * a + 3]))
            return tuple(out)

        accs = lax.fori_loop(0, GRID, tap_body, (nothing,) * 9)
        rep[0:9, cols] = jnp.concatenate(
            [jnp.sum(acc, axis=0, keepdims=True) for acc in accs], axis=0
        )
    ig_o[...] = res[...].astype(BF16)

    sm[:, 72:] = jnp.zeros((sm.shape[0], sm.shape[1] - 72, LANE), F32)
    half = hg_one.shape[0]
    for k in range(slots.nh):
        at = table[slots.head_col + k]
        sm[at, 0:56] = hg_one[k] if k < half else hg_two[k - half]
    for t in range(width // LANE):
        cols = slice(t * LANE, (t + 1) * LANE)
        sm[t, 0:TAPS] = sm[t, 0:TAPS] * mask[:, cols]
        for r in range(ubg.shape[0]):
            sm[t, 52 + r : 53 + r] = ubg[r, 0:1, cols]
        sm[t, 56:72] = rep[:, cols]
    span = small_o.shape[2]
    for u in range(small_o.shape[0]):
        for t in range(width // LANE):
            at = table[slots.up_out + u]
            to = table[slots.head_out + t]
            small_o[at, to] = sm[t, u * span : (u + 1) * span]


def whole(shape):
    return pl.BlockSpec(shape, lambda *_: (0,) * len(shape))


def adam_store(outs, raw, weight, first, second, average, clip, decay):
    grad = raw * clip
    first_new = BETA_FIRST * first + (1.0 - BETA_FIRST) * grad
    second_new = BETA_SECOND * second + (1.0 - BETA_SECOND) * grad * grad
    moment_hat = first_new / (1.0 - BETA_FIRST**STEP)
    second_hat = second_new / (1.0 - BETA_SECOND**STEP)
    weight_new = weight - LEARN_RATE * (
        moment_hat / (jnp.sqrt(second_hat) + ADAM_EPS) + decay * weight
    )
    outs[0][...] = grad
    outs[1][...] = first_new
    outs[2][...] = second_new
    outs[3][...] = weight_new
    outs[4][...] = weight_new.astype(BF16)
    outs[5][...] = AVG_KEEP * average + (1.0 - AVG_KEEP) * weight_new


def adam_kernel(table, shares, one, two, *refs, slots, span):
    ins, norm_o, outs, sm = refs[:24], refs[24], refs[25:61], refs[61]
    tiles = sm.shape[0]
    total = jnp.zeros((1, 1), F32)
    for u in range(slots.up):
        for t in range(tiles):
            share = shares[table[slots.up_in + u], table[slots.head_abs + t]]
            sm[t, u * span : (u + 1) * span] = share[0:span]
            total = total + jnp.sum(share[0:span] * share[0:span], keepdims=True)
            total = total + share[span : span + 1, 0:1]
    norm = jnp.sqrt(total)
    clip = jnp.minimum(1.0, CLIP_NORM / (norm + 1e-06))
    norm_o[...] = norm
    raws = (one[0:3], one[3], two[0], two[1])
    for p, raw in enumerate(raws):
        state = [ref[...] for ref in ins[4 * p : 4 * p + 4]]
        adam_store(outs[6 * p : 6 * p + 6], raw, *state, clip, WEIGHT_DECAY)
    for p, (begin, end) in ((4, (0, 56)), (5, (56, 72))):
        for t in range(tiles):
            cols = slice(t * LANE, (t + 1) * LANE)
            state = [ref[:, cols] for ref in ins[4 * p : 4 * p + 4]]
            to = [ref.at[:, cols] for ref in outs[6 * p : 6 * p + 6]]
            adam_store(to, sm[t, begin:end], *state, clip, 0.0)


def square_sum(values):
    return jnp.sum(values * values)


class Ring:
    def __init__(self, nd, nh):
        self.low = 2 if nd % 2 == 0 else 1
        self.nd, self.nh, self.up = nd, nh, nd // self.low
        dp = lax.axis_index("dp")
        self.mine = (dp % self.low, dp // self.low, lax.axis_index("head"))

    def turn(self, value, stage, k=1):
        axis = "head" if stage == "head" else "dp"
        low, up = self.low, self.up
        if stage == "head":
            pairs = [(i, (i + k) % self.nh) for i in range(self.nh)]
        elif stage == "up":
            pairs = [(i, (i // low + k) % up * low + i % low) for i in range(self.nd)]
        else:
            pairs = [(i, i // low * low + (i % low + k) % low) for i in range(self.nd)]
        return lax.ppermute(value, axis, pairs)

    def gather(self, shard, stage):
        size = self.nh if stage == "head" else self.up
        return jnp.stack([shard] + [self.turn(shard, stage, k) for k in range(1, size)])

    def scatter(self, parts, stage):
        total = parts[0].astype(F32)
        for k in range(1, len(parts)):
            total = total + self.turn(parts[k], stage, k).astype(F32)
        return total

    def swap_sum(self, keep, send):
        return keep.astype(F32) + self.turn(send, "low").astype(F32)


def per_device(
    block_input,
    out_grad,
    kernel_radius,
    qkv_weight,
    qkv_first,
    qkv_second,
    qkv_average,
    proj_weight,
    proj_first,
    proj_second,
    proj_average,
    up_weight,
    up_first,
    up_second,
    up_average,
    down_weight,
    down_first,
    down_second,
    down_average,
    head_params,
    head_first,
    head_second,
    head_average,
    rep_params,
    rep_first,
    rep_second,
    rep_average,
):
    nd, nh = lax.axis_size("dp"), lax.axis_size("head")
    imgs, _, width = block_input.shape
    rows = SEQ * imgs
    span = qkv_weight.shape[0]
    hid = up_weight.shape[1]
    ring = Ring(nd, nh)
    staged = span % 16 == 0 and ring.low == 2
    tiles = width // LANE

    x = block_input.transpose(1, 0, 2).reshape(rows, width)
    cot = out_grad.transpose(1, 0, 2).reshape(rows, width)
    kinds_first = lambda v: v.transpose(1, 0, 2)
    pack_one = jnp.concatenate(
        [kinds_first(qkv_weight).astype(BF16), proj_weight.astype(BF16)[None]], axis=0
    )
    pack_two = jnp.stack([up_weight.astype(BF16), down_weight.astype(BF16)])
    up = ring.up if staged else 4
    slots = Slots(up, nh)
    ups = jnp.arange(up, dtype=jnp.int32)
    heads = jnp.arange(nh, dtype=jnp.int32)
    if staged:
        size = span
        my_low, my_up, z = ring.mine
        parts = [
            (my_up - ups) % up,
            (ups - my_up) % up,
            (nh - heads) % nh,
            (z + heads) % nh,
            (heads - z) % nh,
            (z - heads) % nh,
            my_low[None],
        ]
        gathered_one = ring.gather(ring.gather(pack_one, "head"), "up")
        other_one = ring.turn(gathered_one, "low")
        gathered_two = ring.gather(ring.gather(pack_two, "head"), "up")
        other_two = ring.turn(gathered_two, "low")
    else:
        size = width // (2 * up)
        parts = [ups, ups, heads, heads, heads, heads, jnp.zeros((1,), jnp.int32)]

        def spread(pack):
            kinds = pack.shape[0]
            full = lax.all_gather(pack, ("dp", "head"), axis=0)
            full = full.reshape(nd, nh, kinds, span, -1).transpose(1, 2, 0, 3, 4)
            full = full.reshape(nh, kinds, up, 2, size, -1).transpose(3, 2, 0, 1, 4, 5)
            return full[0], full[1]

        gathered_one, other_one = spread(pack_one)
        gathered_two, other_two = spread(pack_two)
    table = jnp.concatenate([p.astype(jnp.int32) for p in parts])

    shape = jax.ShapeDtypeStruct

    def params(mebibytes, *semantics):
        return pltpu.CompilerParams(
            dimension_semantics=semantics or None, vmem_limit_bytes=mebibytes * 1024 * 1024
        )

    def cost(us):
        return pl.CostEstimate(flops=0, transcendentals=0, bytes_accessed=int(us * 3.0e6))

    def weight_spec(kinds, cols):
        return pl.BlockSpec(
            (up, 1, kinds, size, cols), lambda j, s: (0, s[slots.head_in + j], 0, 0, 0)
        )

    full = whole((rows, width))
    turned = whole((width, rows))
    rp_spec = whole((16, width))
    wide = shape((rows, width), F32)
    low = shape((rows, width), BF16)
    low_turned = shape((width, rows), BF16)

    stream_zero, normed_one, normed_one_t = pl.pallas_call(
        partial(pre_kernel, imgs=imgs),
        out_shape=(wide, low, low_turned),
        scratch_shapes=[pltpu.VMEM((9 * GRID * imgs, width), F32)],
        compiler_params=params(10),
        cost_estimate=cost(9),
        name="pre",
    )(x, rep_params)
    cot_t, cot_sum = pl.pallas_call(
        cot_kernel,
        out_shape=(low_turned, shape((8, width), F32)),
        compiler_params=params(6),
        cost_estimate=cost(2),
        name="cot",
    )(cot)

    head_rows, mask = pl.pallas_call(
        taps_kernel,
        out_shape=(shape(head_params.shape, F32), shape((TAPS, width), F32)),
        in_specs=[
            pl.BlockSpec(memory_space=pltpu.SMEM),
            pl.BlockSpec(memory_space=pltpu.VMEM),
        ],
        compiler_params=params(2),
        cost_estimate=cost(1),
        name="taps",
    )(kernel_radius, head_params)
    bias_up = head_params[TAPS + 3 :].reshape(nh, 1, hid)
    per_head = shape((nh, rows, LANE), F32)
    tile_spec = pl.BlockSpec((1, rows, LANE), lambda j, s: (j, 0, 0))
    padded = pltpu.VMEM((PAD_TOKENS * imgs, LANE), F32)
    framed = pltpu.VMEM((13 * GRID * imgs, LANE), F32)
    w_one = pltpu.VMEM((width, 4 * LANE), BF16)
    hp_spec = pl.BlockSpec((56, LANE), lambda j, s: (0, s[slots.head_col + j]))
    queries, keys_soft, values, conv_val, attended, stream_one, normed_two, normed_two_t = (
        pl.pallas_call(
            partial(attn_kernel, imgs=imgs, slots=slots),
            out_shape=(
                per_head,
                per_head,
                per_head,
                per_head,
                shape((nh, rows, LANE), BF16),
                wide,
                low,
                low_turned,
            ),
            grid_spec=pltpu.PrefetchScalarGridSpec(
                num_scalar_prefetch=1,
                grid=(nh,),
                in_specs=[full, full] + [weight_spec(4, LANE)] * 2 + [hp_spec, rp_spec],
                out_specs=[tile_spec] * 5 + [full, full, turned],
                scratch_shapes=[w_one] + [padded] * 4 + [framed],
            ),
            compiler_params=params(19, "arbitrary"),
            cost_estimate=cost(21),
            name="attn",
        )(table, normed_one, stream_zero, gathered_one, other_one, head_rows, rep_params)
    )

    pair = 1
    two_grads = shape((up, nh, 2, size, hid), BF16)
    two_spec = pl.BlockSpec((up, pair, 2, size, hid), lambda j, s: (0, j, 0, 0, 0))
    all_hidden = shape((nh, 8, hid), F32)

    def resident(dims):
        zeros = (0,) * len(dims)
        return pl.BlockSpec(dims, lambda j, s: zeros, pipeline_mode=pl.Buffered(1))

    def pair_spec(n):
        return pl.BlockSpec(
            (up, 1, 2, size, hid), lambda j, s: (0, s[slots.head_in + pair * j + n], 0, 0, 0)
        )

    pair_specs = [pair_spec(n) for n in range(pair)]
    output, grad_norm_two, keep_two, send_two, bias_grad = pl.pallas_call(
        partial(mlp_kernel, imgs=imgs, slots=slots, hid=hid, heads=pair),
        out_shape=(low, wide, two_grads, two_grads, all_hidden),
        grid_spec=pltpu.PrefetchScalarGridSpec(
            num_scalar_prefetch=1,
            grid=(nh // pair,),
            in_specs=[resident(v) for v in ((rows, width), (width, rows)) * 2 + ((rows, width),)]
            + pair_specs * 2
            + [whole((nh, 1, hid)), rp_spec],
            out_specs=[full, full, two_spec, two_spec, whole((nh, 8, hid))],
            scratch_shapes=[
                pltpu.VMEM((width, 2 * pair * hid), BF16),
                pltpu.VMEM((rows, pair * hid), F32),
                pltpu.VMEM((rows, pair * hid), F32),
                pltpu.VMEM((rows, pair * hid), BF16),
                pltpu.VMEM((rows, pair * hid), BF16),
                pltpu.VMEM((rows, width), F32),
            ],
        ),
        compiler_params=params(26, "arbitrary"),
        cost_estimate=cost(20),
        name="mlp",
    )(
        table,
        normed_two,
        normed_two_t,
        cot,
        cot_t,
        stream_one,
        *[gathered_two] * pair,
        *[other_two] * pair,
        bias_up,
        rep_params,
    )

    grad_one, grad_low, grad_low_t, rep_mid = pl.pallas_call(
        partial(mid_kernel, imgs=imgs),
        out_shape=(wide, low, low_turned, shape((8, width), F32)),
        compiler_params=params(9),
        cost_estimate=cost(4),
        name="mid",
    )(grad_norm_two, stream_one, cot, rep_params)

    cut = nh - 1
    one_spec = pl.BlockSpec((up, 1, 4, size, LANE), lambda j, s: (0, j, 0, 0, 0))

    def attn_back(begin, count, so_far):
        one_grads = shape((up, count, 4, size, LANE), BF16)

        def at_head(j, s):
            return (0, s[slots.head_in + begin + j], 0, 0, 0)

        weights = pl.BlockSpec((up, 1, 4, size, LANE), at_head)
        tile = pl.BlockSpec((1, rows, LANE), lambda j, s: (begin + j, 0, 0))
        taps = pl.BlockSpec((56, LANE), lambda j, s: (0, s[slots.head_col + begin + j]))
        return pl.pallas_call(
            partial(attn_back_kernel, imgs=imgs, slots=slots, begin=begin),
            out_shape=(one_grads, one_grads, wide, shape((count, 56, LANE), F32)),
            grid_spec=pltpu.PrefetchScalarGridSpec(
                num_scalar_prefetch=1,
                grid=(count,),
                in_specs=[turned, full, turned, weights, weights, taps]
                + [tile] * 5
                + [full] * len(so_far),
                out_specs=[
                    one_spec,
                    one_spec,
                    full,
                    pl.BlockSpec((1, 56, LANE), lambda j, s: (j, 0, 0)),
                ],
                scratch_shapes=[w_one]
                + [padded] * 7
                + [framed] * 2
                + [pltpu.VMEM((rows, 3 * LANE), BF16)],
            ),
            compiler_params=params(21, "arbitrary"),
            cost_estimate=cost(7 * count),
            name="attn_back_b" if begin else "attn_back_a",
        )(
            table,
            normed_one_t,
            grad_low,
            grad_low_t,
            gathered_one,
            other_one,
            head_rows,
            queries,
            keys_soft,
            values,
            conv_val,
            attended,
            *so_far,
        )

    keep_a, send_a, grad_part, head_a = attn_back(0, cut, ())
    keep_b, send_b, grad_norm_one, head_b = attn_back(cut, nh - cut, (grad_part,))

    small_rows = 8 * pl.cdiv(72, 8 * up)
    smem = pl.BlockSpec(memory_space=pltpu.SMEM)
    vmem = pl.BlockSpec(memory_space=pltpu.VMEM)
    input_grad, small = pl.pallas_call(
        partial(tail_kernel, imgs=imgs, slots=slots),
        out_shape=(low, shape((up, tiles, small_rows, LANE), F32)),
        in_specs=[smem] + [vmem] * 11,
        scratch_shapes=[
            pltpu.VMEM((9 * GRID * imgs, width), F32),
            pltpu.VMEM((9 * GRID * imgs, width), F32),
            pltpu.VMEM((rows, width), F32),
            pltpu.VMEM((tiles, up * small_rows, LANE), F32),
            pltpu.VMEM((16, width), F32),
        ],
        compiler_params=params(16),
        cost_estimate=cost(9),
        name="tail",
    )(
        table,
        stream_zero,
        grad_one,
        grad_norm_one,
        x,
        rep_params,
        head_a,
        head_b,
        bias_grad,
        rep_mid,
        cot_sum,
        mask,
    )

    if staged:
        two = ring.swap_sum(keep_two, send_two).astype(BF16)
        two = ring.scatter(two, "up").astype(BF16)
        two = ring.scatter(two, "head")
        one_a = ring.swap_sum(keep_a, send_a).astype(BF16)
        one_b = ring.swap_sum(keep_b, send_b).astype(BF16)
        one = ring.scatter(jnp.concatenate([one_a, one_b], axis=1), "up").astype(BF16)
        share = ring.scatter(small, "up").astype(BF16)
        pad = -small_rows % 16
        rider = jnp.concatenate(
            [one.reshape(nh, 4 * size, LANE), jnp.pad(share, ((0, 0), (0, pad), (0, 0)))], axis=1
        )
        rider = ring.scatter(rider, "head")
        one = rider[: 4 * size].reshape(4, size, LANE)
        share = rider[4 * size : 4 * size + small_rows]
        mine = jnp.zeros((8, LANE), F32) + (square_sum(one) + square_sum(two))
        shares = jnp.concatenate([share, mine], axis=0)
        shares = ring.swap_sum(shares, shares)
        shares = ring.gather(ring.gather(shares, "head"), "up")
    else:

        def owned(even, odd):
            full = jnp.stack([even, odd], axis=1)
            kinds = full.shape[3]
            full = full.transpose(2, 3, 0, 1, 4, 5).reshape(nh, kinds, nd, span, -1)
            full = full.transpose(2, 0, 1, 3, 4).reshape(nd * nh, kinds, span, -1)
            return lax.psum_scatter(full, ("dp", "head"), scatter_dimension=0).astype(F32)

        two = owned(keep_two, send_two)
        one = owned(
            jnp.concatenate([keep_a, keep_b], axis=1), jnp.concatenate([send_a, send_b], axis=1)
        )
        small_sum, mat_total = lax.psum(
            (small, square_sum(one) + square_sum(two)), ("dp", "head")
        )
        first_cell = (lax.broadcasted_iota(jnp.int32, (up, tiles, 8, LANE), 0) == 0) & (
            lax.broadcasted_iota(jnp.int32, (up, tiles, 8, LANE), 1) == 0
        )
        mine = jnp.where(first_cell, mat_total, F32(0.0))
        shares = jnp.concatenate([small_sum, mine], axis=2)

    states = (
        *(kinds_first(v) for v in (qkv_weight, qkv_first, qkv_second, qkv_average)),
        *(proj_weight, proj_first, proj_second, proj_average),
        *(up_weight, up_first, up_second, up_average),
        *(down_weight, down_first, down_second, down_average),
        *(head_params, head_first, head_second, head_average),
        *(rep_params, rep_first, rep_second, rep_average),
    )
    results = []
    for p in range(6):
        like = states[4 * p].shape
        results += [shape(like, BF16 if k == 4 else F32) for k in range(6)]
    norm, *outs = pl.pallas_call(
        partial(adam_kernel, slots=slots, span=small_rows),
        out_shape=(shape((1, 1), F32), *results),
        in_specs=[smem] + [vmem] * 27,
        scratch_shapes=[pltpu.VMEM((tiles, up * small_rows, LANE), F32)],
        compiler_params=params(10),
        cost_estimate=cost(4),
        name="adam",
    )(table, shares, one, two, *states)
    outs[0:6] = [kinds_first(v) for v in outs[0:6]]

    def by_image(v):
        return v.reshape(SEQ, imgs, width).transpose(1, 0, 2)

    return (by_image(output), by_image(input_grad), norm.reshape(()), *outs)


def solution(mesh):
    tokens = P(("dp", "head"), None, None)
    qkv = P("dp", None, "head")
    mat = P("dp", "head")
    in_specs = (tokens, tokens, P()) + (qkv,) * 4 + (mat,) * 12 + (P(),) * 8
    out_specs = (tokens, tokens, P()) + (qkv,) * 6 + (mat,) * 18 + (P(),) * 12

    return jax.shard_map(
        per_device, mesh=mesh, in_specs=in_specs, out_specs=out_specs, check_vma=False
    )
```
